32 devices in a mesh: grp: 4 (over y, core), blk: 8 (over z, x).
Axes of the slice: x: 2, y: 2, z: 4, core: 2. Of those that a mesh axis runs over, the one named last changes fastest.
Arguments:
- features: bfloat16 [4096, 128], P(('grp', 'blk')), may hold values from -6 to 6
- col_scale: float32 [4096], P(('grp', 'blk')), may hold values from 0.5 to 2
- row_scale: float32 [4096], P(('grp', 'blk')), may hold values from 0.5 to 2
- tiles: bfloat16 [1024, 128, 128], P(('grp', 'blk')), may hold values from 0 to 0.03125
- tile_cols: int32 [1024], P(('grp', 'blk')), may hold values from 0 to 3
- weight: bfloat16 [128, 256], replicated, may hold values from -0.5 to 0.5
- cotangent: bfloat16 [4096, 256], P(('grp', 'blk')), may hold values from -0.1875 to 0.1875
- train_mask: int32 [4096], P(('grp', 'blk')), may hold values 0 or 1
Outputs:
- hidden: bfloat16 [4096, 256], P(('grp', 'blk'))
- weight_grad: float32 [128, 256], replicated
The draws below stay inside these ranges and needn't reach their ends.
All inputs are finite; a program needn't handle non-finite values. No bound on the sum of `train_mask` on one device may be relied on, other than what follows from the above.
Results may differ from the reference program's by a relative error of at most 0.0054.
Values may be sent and summed in bfloat16 or wider, within the bound.
A program may use at most 128 MiB of HBM per device.

```python
import math
import jax
import jax.numpy as jnp
from jax import lax

FIN = 128
HID = 256
TILE = 128
TPR = 4
NODE_DEV = 128
NODES = 4096
COL_BLOCKS = 4
TILES_ALL = 1024
N_GRP = 4
N_BLK = 8


def plant(drawn, own_key, least, largest):
    longest = drawn.shape.index(max(drawn.shape))
    spots = []
    for shift in (0, 1):
        where = [jax.random.randint(jax.random.fold_in(own_key, axis), (), 0, length) for axis, length in enumerate(drawn.shape)]
        where[longest] = (where[longest] + shift) % drawn.shape[longest]
        spots.append(tuple(where))
    return drawn.at[spots[0]].set(least).at[spots[1]].set(largest)


def shard_levels(key, extent, pieces, smallest, largest):
    gain, own = 1.0, jax.random.fold_in(key, 6)
    for dim, blocks in pieces:
        steps = jnp.exp(jax.random.uniform(jax.random.fold_in(own, dim), (blocks,), jnp.float32, smallest / len(pieces), largest / len(pieces)))
        gain = gain * jnp.repeat(steps, extent[dim] // blocks).reshape([-1 if axis == dim else 1 for axis in range(len(extent))])
    return gain


def scatter_about(key, dims, deviation, most, split=(), dtype=jnp.bfloat16):
    array = jax.random.normal(key, dims, jnp.float32) * deviation
    if len(split) > 0:
        array = shard_levels(key, dims, split, -0.22, 0.18) * array
    return jnp.clip(array, min=-most, max=most).astype(dtype)


def setup_inputs(seed: int = 0) -> dict:
    keys = jax.random.split(jax.random.key(seed), 9)
    return {
        "features": scatter_about(keys[0], (NODES, FIN), 1.0, 6.0, ((0, 32),)),
        "col_scale": jnp.clip(jnp.exp(math.log(2.0) - 1.3862944 * jax.random.uniform(keys[1], (NODES,), jnp.float32) ** shard_levels(keys[1], (NODES,), ((0, 32),), -0.2, 0.2)), 0.5, 2.0),
        "row_scale": jnp.clip(jnp.exp(math.log(2.0) - 1.3862944 * jax.random.uniform(keys[2], (NODES,), jnp.float32) ** shard_levels(keys[2], (NODES,), ((0, 32),), -0.2, 0.2)), 0.5, 2.0),
        "tiles": jnp.clip(0.03125 * jax.random.uniform(keys[3], (TILES_ALL, TILE, TILE), jnp.float32) ** shard_levels(keys[3], (TILES_ALL, TILE, TILE), ((0, 32),), -0.2, 0.2), 0.0, 0.03125).astype(jnp.bfloat16),
        "tile_cols": plant(jax.random.randint(keys[4], (TILES_ALL,), 0, COL_BLOCKS), jax.random.fold_in(keys[4], 1), 0, COL_BLOCKS - 1).astype(jnp.int32),
        "weight": scatter_about(keys[5], (FIN, HID), FIN ** -0.5, 0.5),
        "cotangent": scatter_about(keys[6], (NODES, HID), (2 * NODES ** -0.5), 0.1875, ((0, 32),)),
        "train_mask": plant((jax.random.randint(keys[7], (NODES,), 0, 4) < 1).astype(jnp.int32), jax.random.fold_in(keys[7], 1), 0, 1),
    }


def activate(values):
    return jax.nn.gelu(values, approximate=True)

def reference(features, col_scale, row_scale, tiles, tile_cols, weight, cotangent, train_mask):
    per_dev = NODE_DEV // TILE
    scaled = (col_scale[:, None] * features.astype(jnp.float32)).astype(jnp.bfloat16)
    blocks = scaled.reshape(N_GRP, N_BLK, per_dev, TILE, FIN)
    tile_view = tiles.reshape(N_GRP, N_BLK, N_BLK * per_dev * TPR, TILE, TILE)
    col_view = tile_cols.reshape(N_GRP, N_BLK, N_BLK * per_dev * TPR)

    def group(gindex):

        def step(total, bindex):
            source = lax.dynamic_index_in_dim(blocks, bindex, 1, keepdims=False)
            source = source.reshape(N_GRP * per_dev, TILE, FIN)
            picked = source[col_view[gindex, bindex]].astype(jnp.float32)
            picked = picked.reshape(N_BLK * per_dev, TPR, TILE, FIN)
            piece = tile_view[gindex, bindex].astype(jnp.float32).reshape(N_BLK * per_dev, TPR, TILE, TILE)
            return (total + jnp.einsum('rkij,rkjf->rif', piece, picked), None)
        start = jnp.zeros((N_BLK * per_dev, TILE, FIN), jnp.float32)
        total, _ = lax.scan(step, start, jnp.arange(N_BLK))
        return total
    aggregate = lax.map(group, jnp.arange(N_GRP)).reshape(NODES, FIN)
    mixed = row_scale[:, None] * aggregate
    pre = jnp.dot(mixed, weight.astype(jnp.float32), precision=lax.Precision.HIGHEST)
    hidden, backward = jax.vjp(activate, pre)
    masked_grad = cotangent.astype(jnp.float32) * train_mask.astype(jnp.float32)[:, None]
    delta = backward(masked_grad)[0]
    weight_grad = jnp.dot(mixed.T, delta, precision=lax.Precision.HIGHEST)
    return (hidden.astype(jnp.bfloat16), weight_grad)
```

```python
import functools
import math

import jax
import jax.numpy as jnp
from jax import lax
from jax.experimental import pallas as pl
from jax.experimental.pallas import tpu as pltpu
from jax.sharding import PartitionSpec as P

TPR = 4
ROOT = math.sqrt(2.0 / math.pi)
CUBE = 0.044715
MESH = pl.DeviceIdType.MESH
F32 = jnp.float32
BF16 = jnp.bfloat16
GRAD_LINK = BF16
VLIM = 32 * 1024 * 1024


def far_first(count):
    return sorted(range(1, count), key=lambda step: abs(2 * step - count))


def split(value):
    high = value.astype(BF16)
    return high, (value - high.astype(F32)).astype(BF16)


def down_rows(row, width):
    return jnp.broadcast_to(row, (width, row.shape[1])).T


def kernel(n_grp, n_blk, pieces, cols_in, features, col_scale, row_scale, tiles, weight, cotangent,
           train_mask, packed, cols, feat, cscale, rscale, mask, wgt, cot, held, sources,
           mine, outgoing, arrived, grad_parts, grad_in, in_sems, tile_sems, src_send,
           src_recv, part_send, part_recv, grad_sems):
    top = feat.shape[0] // 8
    g, b = lax.axis_index("grp"), lax.axis_index("blk")
    order = far_first(n_blk) + [0]

    def grp_peer(step):
        return lax.rem(g + step, n_grp)

    def blk_peer(step):
        return lax.rem(b + step, n_blk)

    def load(source, target, sem):
        copy = pltpu.make_async_copy(source, target, sem)
        copy.start()
        return copy

    first = [load(features, feat, in_sems.at[0]), load(col_scale, cscale, in_sems.at[1])]

    cols_load = load(cols_in, cols, in_sems.at[6])

    barrier = pltpu.get_barrier_semaphore()
    for step in range(1, n_grp):
        pl.semaphore_signal(barrier, inc=1, device_id=(grp_peer(step), b), device_id_type=MESH)
    for step in range(1, n_blk):
        pl.semaphore_signal(barrier, inc=1, device_id=(g, blk_peer(step)), device_id_type=MESH)

    tile_loads = []
    for spot, step in enumerate(order):
        rows = pl.ds(blk_peer(step) * TPR, TPR)
        tile_loads.append(load(tiles.at[rows], held.at[rows], tile_sems.at[spot]))
    late = [
        load(row_scale, rscale, in_sems.at[2]),
        load(train_mask, mask, in_sems.at[3]),
        load(weight, wgt, in_sems.at[4]),
        load(cotangent, cot, in_sems.at[5]),
    ]

    for copy in first:
        copy.wait()
    sources[g] = (down_rows(cscale[...], feat.shape[1]) * feat[...].astype(F32)).astype(BF16)
    pl.semaphore_wait(barrier, n_grp + n_blk - 2)

    src_copies = []
    for step in range(1, n_grp):
        copy = pltpu.make_async_remote_copy(
            src_ref=sources.at[g], dst_ref=sources.at[g],
            send_sem=src_send.at[step - 1], recv_sem=src_recv.at[step - 1],
            device_id=(grp_peer(step), b), device_id_type=MESH)
        copy.start()
        src_copies.append(copy)
    cols_load.wait()
    for copy in tile_loads:
        copy.wait()
    for copy in src_copies:
        copy.wait()

    def partial(block):
        base = block * TPR
        left = jnp.concatenate([held[base + k] for k in range(TPR)], axis=1)
        right = jnp.concatenate([sources[cols[base + k]] for k in range(TPR)], axis=0)
        return jnp.dot(left, right, preferred_element_type=F32)

    part_copies = []
    for spot, step in enumerate(order[:-1]):
        block = blk_peer(step)
        outgoing[spot] = partial(block).astype(BF16)
        copy = pltpu.make_async_remote_copy(
            src_ref=outgoing.at[spot], dst_ref=arrived.at[spot],
            send_sem=part_send.at[spot], recv_sem=part_recv.at[spot],
            device_id=(g, block), device_id_type=MESH)
        copy.start()
        part_copies.append(copy)
    mine[...] = partial(b)

    for copy in late:
        copy.wait()
    row_full = down_rows(rscale[...], feat.shape[1])
    mask_full = down_rows(mask[...].astype(F32), cot.shape[1] // 2)
    masked = cot[...].astype(F32) * jnp.concatenate([mask_full, mask_full], axis=1)

    total = mine[...]
    for spot, copy in reversed(list(enumerate(part_copies))):
        copy.wait()
        total = total + arrived[spot].astype(F32)
    mixed = row_full * total

    high, low = split(mixed)
    w = wgt[...]
    pre = jnp.dot(jnp.concatenate([high, low], axis=1), jnp.concatenate([w, w], axis=0),
                  preferred_element_type=F32)
    square = pre * pre
    bent = jnp.tanh(ROOT * pre * (1.0 + CUBE * square))
    half = 0.5 * (1.0 + bent)
    hidden = (pre * half).astype(packed.dtype)
    for piece in range(top):
        packed[piece] = hidden[piece * 8:piece * 8 + 8]
    slope = half + 0.5 * pre * (1.0 - bent * bent) * (ROOT * (1.0 + 3.0 * CUBE * square))
    delta = slope * masked

    high_t, low_t = split(mixed.T)
    d_high, d_low = split(delta)
    grad = jnp.dot(jnp.concatenate([high_t, low_t, high_t], axis=1),
                   jnp.concatenate([d_high, d_high, d_low], axis=0), preferred_element_type=F32)
    if not pieces:
        for piece in range(grad.shape[0] // 8):
            packed[top + piece] = grad[piece * 8:piece * 8 + 8]
        return

    n = n_grp * n_blk
    me = g * n_blk + b
    span, first_blk = n_blk // 2, n_blk // 4
    owners = n_grp * span
    owner = (b >= first_blk) & (b < first_blk + span)
    seat = g * span + (b - first_blk)
    for piece in range(owners):
        grad_parts[piece] = grad[piece * 8:piece * 8 + 8].astype(GRAD_LINK)

    def scatter(step, _):
        to = lax.rem(me + step, owners)
        to_g, to_b = to // span, first_blk + lax.rem(to, span)

        @pl.when(to_g * n_blk + to_b != me)
        def _():
            pltpu.make_async_remote_copy(
                src_ref=grad_parts.at[to], dst_ref=grad_in.at[me],
                send_sem=grad_sems.at[0], recv_sem=grad_sems.at[1],
                device_id=(to_g, to_b), device_id_type=MESH).start()
        return 0

    lax.fori_loop(0, owners, scatter, 0)
    some = grad_parts.at[pl.ds(0, owners - 1)]

    @pl.when(owner)
    def _():
        grad_in[me] = grad_parts[seat]
        others = grad_in.at[pl.ds(0, n - 1)]
        pltpu.make_async_copy(others, others, grad_sems.at[1]).wait()
        packed[top + seat] = jnp.sum(grad_in[...].astype(F32), axis=0).astype(GRAD_LINK)

        def gather(step, _):
            to = lax.rem(me + step, n)
            pltpu.make_async_remote_copy(
                src_ref=packed.at[top + seat], dst_ref=packed.at[top + seat],
                send_sem=grad_sems.at[2], recv_sem=grad_sems.at[3],
                device_id=(to // n_blk, lax.rem(to, n_blk)), device_id_type=MESH).start()
            return 0

        lax.fori_loop(1, n, gather, 0)
        pltpu.make_async_copy(some, some, grad_sems.at[0]).wait()
        pltpu.make_async_copy(some, some, grad_sems.at[3]).wait()
        pltpu.make_async_copy(others, others, grad_sems.at[2]).wait()

    @pl.when(jnp.logical_not(owner))
    def _():
        pltpu.make_async_copy(grad_parts, grad_parts, grad_sems.at[0]).wait()
        pltpu.make_async_copy(grad_parts, grad_parts, grad_sems.at[3]).wait()


def shards(n_grp, n_blk, features, col_scale, row_scale, tiles, tile_cols, weight, cotangent, train_mask):
    nodes, fin = features.shape
    hid_width = weight.shape[1]
    tile = tiles.shape[1]
    n = n_grp * n_blk
    pieces = n_grp * (n_blk // 2) * 8 == fin
    hbm = pl.BlockSpec(memory_space=pltpu.HBM)
    if pieces:
        spare, landing = (fin // 8, 8, hid_width), (n, 8, hid_width)
    else:
        spare = landing = (1, 8, 128)
    out_type = BF16 if pieces else F32
    hbm = pl.BlockSpec(memory_space=pltpu.HBM)
    if pieces:
        spare, landing = (fin // 8, 8, hid_width), (n, 8, hid_width)
    else:
        spare = landing = (1, 8, 128)
    grad_type = GRAD_LINK if pieces else F32
    grad_shape = jax.ShapeDtypeStruct((fin, hid_width), grad_type)
    dma = pltpu.SemaphoreType.DMA
    packed = pl.pallas_call(
        functools.partial(kernel, n_grp, n_blk, pieces),
        out_shape=pltpu.VMEM(((nodes + fin) // 8, 8, hid_width), out_type),
        in_specs=[hbm] * 8,
        out_specs=pl.BlockSpec(memory_space=pltpu.VMEM),
        scratch_shapes=[
            pltpu.SMEM(tile_cols.shape, jnp.int32),
            pltpu.VMEM((nodes, fin), BF16),
            pltpu.VMEM((1, nodes), F32),
            pltpu.VMEM((1, nodes), F32),
            pltpu.VMEM((1, nodes), jnp.int32),
            pltpu.VMEM((fin, hid_width), BF16),
            pltpu.VMEM((nodes, hid_width), BF16),
            pltpu.VMEM(tiles.shape, BF16),
            pltpu.VMEM((n_grp, tile, fin), BF16),
            pltpu.VMEM((tile, fin), F32),
            pltpu.VMEM((n_blk - 1, tile, fin), BF16),
            pltpu.VMEM((n_blk - 1, tile, fin), BF16),
            pltpu.VMEM(spare, GRAD_LINK),
            pltpu.VMEM(landing, GRAD_LINK),
            dma((7,)), dma((n_blk,)), dma((n_grp - 1,)), dma((n_grp - 1,)),
            dma((n_blk - 1,)), dma((n_blk - 1,)), dma((4,)),
        ],
        compiler_params=pltpu.CompilerParams(
            collective_id=0, has_side_effects=True, vmem_limit_bytes=VLIM),
    )(*[pltpu.with_memory_space_constraint(x, pltpu.HBM) for x in (
        tile_cols, features, col_scale.reshape(1, nodes), row_scale.reshape(1, nodes), tiles, weight,
        cotangent, train_mask.reshape(1, nodes))])
    hidden, grad = packed[:nodes // 8].reshape(nodes, hid_width).astype(BF16), packed[nodes // 8:].reshape(fin, hid_width).astype(F32)
    if not pieces:
        grad = lax.psum(grad, ("grp", "blk"))
    return hidden, grad


def solution(mesh):
    in_specs = (
        P(("grp", "blk"), None),
        P(("grp", "blk")),
        P(("grp", "blk")),
        P(("grp", "blk"), None, None),
        P(("grp", "blk")),
        P(),
        P(("grp", "blk"), None),
        P(("grp", "blk")),
    )
    out_specs = (P(("grp", "blk"), None), P())
    body = functools.partial(shards, mesh.shape["grp"], mesh.shape["blk"])
    return jax.shard_map(body, mesh=mesh, in_specs=in_specs, out_specs=out_specs, check_vma=False)
```

```python
import functools
import math

import jax
import jax.numpy as jnp
from jax import lax
from jax.experimental import pallas as pl
from jax.experimental.pallas import tpu as pltpu
from jax.sharding import PartitionSpec as P

TPR = 4
ROOT = math.sqrt(2.0 / math.pi)
CUBE = 0.044715
MESH = pl.DeviceIdType.MESH
F32 = jnp.float32
BF16 = jnp.bfloat16
GRAD_LINK = BF16
VLIM = 32 * 1024 * 1024
GATHER = [4 * step + turn for step in (5, 4, 7, 6, 3, 2, 1, 0) for turn in (3, 2, 1, 0) if step or turn]


def far_first(count):
    return sorted(range(1, count), key=lambda step: abs(2 * step - count))


def split(value):
    high = value.astype(BF16)
    return high, (value - high.astype(F32)).astype(BF16)


def down_rows(row, width):
    return jnp.broadcast_to(row, (width, row.shape[1])).T


def kernel(n_grp, n_blk, pieces, cols_in, features, col_scale, row_scale, tiles, weight, cotangent,
           train_mask, packed, cols, feat, cscale, rscale, mask, wgt, cot, held, sources,
           mine, outgoing, arrived, grad_parts, grad_in, in_sems, tile_sems, src_send,
           src_recv, part_send, part_recv, grad_sems, greet_sems):
    top = feat.shape[0] // 8
    g, b = lax.axis_index("grp"), lax.axis_index("blk")
    near = pieces and n_blk == 8
    last_row = n_blk // 2 - 1
    row, side = b // 2, lax.rem(b, 2)
    order = list(range(n_blk - 1, -1, -1)) if near else far_first(n_blk) + [0]

    def flip(index, mask):
        out, weight = 0, 1
        while weight <= mask:
            bit = lax.rem(index // weight, 2)
            out = out + weight * (1 - 2 * bit) * (mask // weight % 2)
            weight *= 2
        return index + out

    def grp_peer(step):
        return flip(g, step) if near else lax.rem(g + step, n_grp)

    hemi = row // 2
    rows_near = (row, row + 1 - 2 * lax.rem(row, 2), 2 - hemi, 3 * (1 - hemi))

    def blk_peer(step):
        if near:
            return 2 * rows_near[step // 2] + (1 - side if step % 2 else side)
        return lax.rem(b + step, n_blk)

    def load(source, target, sem):
        copy = pltpu.make_async_copy(source, target, sem)
        copy.start()
        return copy

    def greet(sem):
        pl.semaphore_signal(sem, inc=1, device_id=(g, b + 1 - 2 * side), device_id_type=MESH)

        @pl.when(row > 0)
        def _():
            pl.semaphore_signal(sem, inc=1, device_id=(g, b - 2), device_id_type=MESH)

        @pl.when(row < last_row)
        def _():
            pl.semaphore_signal(sem, inc=1, device_id=(g, b + 2), device_id_type=MESH)

    greeters = 1 + jnp.minimum(row, 1) + jnp.minimum(last_row - row, 1)

    barrier = pltpu.get_barrier_semaphore()
    for step in range(1, n_grp):
        pl.semaphore_signal(barrier, inc=1, device_id=(grp_peer(step), b), device_id_type=MESH)
    if near:
        greet(barrier)
    else:
        for step in range(1, n_blk):
            pl.semaphore_signal(barrier, inc=1, device_id=(g, blk_peer(step)), device_id_type=MESH)

    first = [load(features, feat, in_sems.at[0]), load(col_scale, cscale, in_sems.at[1])]

    cols_load = load(cols_in, cols, in_sems.at[6])

    tile_loads = []
    for spot, step in enumerate(order):
        rows = pl.ds(blk_peer(step) * TPR, TPR)
        tile_loads.append(load(tiles.at[rows], held.at[rows], tile_sems.at[spot]))
    late = [
        load(row_scale, rscale, in_sems.at[2]),
        load(train_mask, mask, in_sems.at[3]),
        load(weight, wgt, in_sems.at[4]),
        load(cotangent, cot, in_sems.at[5]),
    ]

    for copy in first:
        copy.wait()
    sources[g] = (down_rows(cscale[...], feat.shape[1]) * feat[...].astype(F32)).astype(BF16)
    if near:
        pl.semaphore_wait(barrier, n_grp - 1 + greeters)
    else:
        pl.semaphore_wait(barrier, n_grp + n_blk - 2)

    src_copies = []
    for step in range(1, n_grp):
        copy = pltpu.make_async_remote_copy(
            src_ref=sources.at[g], dst_ref=sources.at[g],
            send_sem=src_send.at[step - 1], recv_sem=src_recv.at[step - 1],
            device_id=(grp_peer(step), b), device_id_type=MESH)
        copy.start()
        src_copies.append(copy)
    if near:
        greet(greet_sems.at[0])
        pl.semaphore_wait(greet_sems.at[0], greeters)
        pl.semaphore_signal(greet_sems.at[1], inc=1, device_id=(g, flip(b, 4)), device_id_type=MESH)
        pl.semaphore_wait(greet_sems.at[1], 1)
    cols_load.wait()
    for copy in tile_loads:
        copy.wait()
    for copy in src_copies:
        copy.wait_recv()

    def partial(block):
        base = block * TPR
        left = jnp.concatenate([held[base + k] for k in range(TPR)], axis=1)
        right = jnp.concatenate([sources[cols[base + k]] for k in range(TPR)], axis=0)
        return jnp.dot(left, right, preferred_element_type=F32)

    part_copies = []
    for spot, step in enumerate(order[:-1]):
        block = blk_peer(step)
        outgoing[spot] = partial(block).astype(BF16)
        copy = pltpu.make_async_remote_copy(
            src_ref=outgoing.at[spot], dst_ref=arrived.at[b],
            send_sem=part_send.at[spot], recv_sem=part_recv.at[b],
            device_id=(g, block), device_id_type=MESH)
        copy.start()
        part_copies.append(copy)
    mine[...] = partial(b)

    for copy in late:
        copy.wait()
    row_full = down_rows(rscale[...], feat.shape[1])
    mask_full = down_rows(mask[...].astype(F32), cot.shape[1] // 2)
    masked = cot[...].astype(F32) * jnp.concatenate([mask_full, mask_full], axis=1)

    total = mine[...]
    for step in reversed(order[:-1]):
        block = blk_peer(step)
        slot = arrived.at[block]
        pltpu.make_async_copy(slot, slot, part_recv.at[block]).wait()
        total = total + slot[...].astype(F32)
    mixed = row_full * total

    high, low = split(mixed)
    w = wgt[...]
    pre = jnp.dot(jnp.concatenate([high, low], axis=1), jnp.concatenate([w, w], axis=0),
                  preferred_element_type=F32)
    square = pre * pre
    bent = jnp.tanh(ROOT * pre * (1.0 + CUBE * square))
    half = 0.5 * (1.0 + bent)
    hidden = (pre * half).astype(packed.dtype)
    for piece in range(top):
        packed[piece] = hidden[piece * 8:piece * 8 + 8]
    slope = half + 0.5 * pre * (1.0 - bent * bent) * (ROOT * (1.0 + 3.0 * CUBE * square))
    delta = slope * masked

    high_t, low_t = split(mixed.T)
    d_high, d_low = split(delta)
    grad = jnp.dot(jnp.concatenate([high_t, low_t, high_t], axis=1),
                   jnp.concatenate([d_high, d_high, d_low], axis=0), preferred_element_type=F32)
    if not pieces:
        for piece in range(grad.shape[0] // 8):
            packed[top + piece] = grad[piece * 8:piece * 8 + 8]
        for copy in src_copies + part_copies:
            copy.wait_send()
        return

    n = n_grp * n_blk
    me = g * n_blk + b
    span, first_blk = n_blk // 2, n_blk // 4
    owners = n_grp * span
    owner = (b >= first_blk) & (b < first_blk + span)
    seat = g * span + (b - first_blk)
    for piece in range(owners):
        grad_parts[piece] = grad[piece * 8:piece * 8 + 8].astype(GRAD_LINK)

    for mid in (1 - hemi, hemi):
        for turn in reversed(range(2 * n_grp)):
            to_g, to_b = flip(g, turn % n_grp), 2 * (mid + 1) + lax.rem(side + turn // n_grp, 2)
            to = to_g * span + (to_b - first_blk)

            def scatter(to=to, to_g=to_g, to_b=to_b):
                pltpu.make_async_remote_copy(
                    src_ref=grad_parts.at[to], dst_ref=grad_in.at[me],
                    send_sem=grad_sems.at[0], recv_sem=grad_sems.at[1],
                    device_id=(to_g, to_b), device_id_type=MESH).start()

            if turn == 0:
                pl.when(to_b != b)(scatter)
            else:
                scatter()
    some = grad_parts.at[pl.ds(0, owners - 1)]

    @pl.when(owner)
    def _():
        grad_in[me] = grad_parts[seat]
        others = grad_in.at[pl.ds(0, n - 1)]
        pltpu.make_async_copy(others, others, grad_sems.at[1]).wait()
        packed[top + seat] = jnp.sum(grad_in[...].astype(F32), axis=0).astype(GRAD_LINK)
        for turn in GATHER:
            pltpu.make_async_remote_copy(
                src_ref=packed.at[top + seat], dst_ref=packed.at[top + seat],
                send_sem=grad_sems.at[2], recv_sem=grad_sems.at[3],
                device_id=(flip(g, turn % n_grp), flip(b, turn // n_grp)), device_id_type=MESH).start()
        pltpu.make_async_copy(some, some, grad_sems.at[3]).wait()
        pltpu.make_async_copy(some, some, grad_sems.at[0]).wait()
        pltpu.make_async_copy(others, others, grad_sems.at[2]).wait()

    @pl.when(jnp.logical_not(owner))
    def _():
        pltpu.make_async_copy(grad_parts, grad_parts, grad_sems.at[3]).wait()
        pltpu.make_async_copy(grad_parts, grad_parts, grad_sems.at[0]).wait()

    for copy in src_copies + part_copies:
        copy.wait_send()


def shards(n_grp, n_blk, features, col_scale, row_scale, tiles, tile_cols, weight, cotangent, train_mask):
    nodes, fin = features.shape
    hid_width = weight.shape[1]
    tile = tiles.shape[1]
    n = n_grp * n_blk
    pieces = n_grp * (n_blk // 2) * 8 == fin
    hbm = pl.BlockSpec(memory_space=pltpu.HBM)
    if pieces:
        spare, landing = (fin // 8, 8, hid_width), (n, 8, hid_width)
    else:
        spare = landing = (1, 8, 128)
    out_type = BF16 if pieces else F32
    hbm = pl.BlockSpec(memory_space=pltpu.HBM)
    if pieces:
        spare, landing = (fin // 8, 8, hid_width), (n, 8, hid_width)
    else:
        spare = landing = (1, 8, 128)
    grad_type = GRAD_LINK if pieces else F32
    grad_shape = jax.ShapeDtypeStruct((fin, hid_width), grad_type)
    dma = pltpu.SemaphoreType.DMA
    packed = pl.pallas_call(
        functools.partial(kernel, n_grp, n_blk, pieces),
        out_shape=pltpu.VMEM(((nodes + fin) // 8, 8, hid_width), out_type),
        in_specs=[hbm] * 8,
        out_specs=pl.BlockSpec(memory_space=pltpu.VMEM),
        scratch_shapes=[
            pltpu.SMEM(tile_cols.shape, jnp.int32),
            pltpu.VMEM((nodes, fin), BF16),
            pltpu.VMEM((1, nodes), F32),
            pltpu.VMEM((1, nodes), F32),
            pltpu.VMEM((1, nodes), jnp.int32),
            pltpu.VMEM((fin, hid_width), BF16),
            pltpu.VMEM((nodes, hid_width), BF16),
            pltpu.VMEM(tiles.shape, BF16),
            pltpu.VMEM((n_grp, tile, fin), BF16),
            pltpu.VMEM((tile, fin), F32),
            pltpu.VMEM((n_blk - 1, tile, fin), BF16),
            pltpu.VMEM((n_blk, tile, fin), BF16),
            pltpu.VMEM(spare, GRAD_LINK),
            pltpu.VMEM(landing, GRAD_LINK),
            dma((7,)), dma((n_blk,)), dma((n_grp - 1,)), dma((n_grp - 1,)),
            dma((n_blk - 1,)), dma((n_blk,)), dma((4,)),
            pltpu.SemaphoreType.REGULAR((2,)),
        ],
        compiler_params=pltpu.CompilerParams(
            collective_id=0, has_side_effects=True, vmem_limit_bytes=VLIM),
    )(*[pltpu.with_memory_space_constraint(x, pltpu.HBM) for x in (
        tile_cols, features, col_scale.reshape(1, nodes), row_scale.reshape(1, nodes), tiles, weight,
        cotangent, train_mask.reshape(1, nodes))])
    hidden, grad = packed[:nodes // 8].reshape(nodes, hid_width).astype(BF16), packed[nodes // 8:].reshape(fin, hid_width).astype(F32)
    if not pieces:
        grad = lax.psum(grad, ("grp", "blk"))
    return hidden, grad


def solution(mesh):
    in_specs = (
        P(("grp", "blk"), None),
        P(("grp", "blk")),
        P(("grp", "blk")),
        P(("grp", "blk"), None, None),
        P(("grp", "blk")),
        P(),
        P(("grp", "blk"), None),
        P(("grp", "blk")),
    )
    out_specs = (P(("grp", "blk"), None), P())
    body = functools.partial(shards, mesh.shape["grp"], mesh.shape["blk"])
    return jax.shard_map(body, mesh=mesh, in_specs=in_specs, out_specs=out_specs, check_vma=False)
```

```python
import functools
import math

import jax
import jax.numpy as jnp
from jax import lax
from jax.experimental import pallas as pl
from jax.experimental.pallas import tpu as pltpu
from jax.sharding import PartitionSpec as P

TPR = 4
ROOT = math.sqrt(2.0 / math.pi)
CUBE = 0.044715
MESH = pl.DeviceIdType.MESH
F32 = jnp.float32
BF16 = jnp.bfloat16
GRAD_LINK = BF16
VLIM = 32 * 1024 * 1024
CUT = 48
GATHER = [4 * step + turn for step in (5, 4, 7, 6, 3, 2, 1, 0) for turn in (3, 2, 1, 0) if step or turn]


def far_first(count):
    return sorted(range(1, count), key=lambda step: abs(2 * step - count))


def split(value):
    high = value.astype(BF16)
    return high, (value - high.astype(F32)).astype(BF16)


def down_rows(row, width):
    return jnp.broadcast_to(row, (width, row.shape[1])).T


def kernel(n_grp, n_blk, pieces, cols_in, features, col_scale, row_scale, tiles, weight, cotangent,
           train_mask, packed, cols, feat, cscale, rscale, mask, wgt, cot, held, sources,
           mine, outgoing, arrived, grad_parts, grad_in, in_sems, tile_sems, src_send,
           src_recv, part_send, part_recv, grad_sems, greet_sems,
           handed, kept, hand_sem):
    top = feat.shape[0] // 8
    g, b = lax.axis_index("grp"), lax.axis_index("blk")
    near = pieces and n_blk == 8
    last_row = n_blk // 2 - 1
    row, side = b // 2, lax.rem(b, 2)
    order = list(range(n_blk - 1, -1, -1)) if near else far_first(n_blk) + [0]

    def flip(index, mask):
        out, weight = 0, 1
        while weight <= mask:
            bit = lax.rem(index // weight, 2)
            out = out + weight * (1 - 2 * bit) * (mask // weight % 2)
            weight *= 2
        return index + out

    def grp_peer(step):
        return flip(g, step) if near else lax.rem(g + step, n_grp)

    hemi = row // 2
    rows_near = (row, row + 1 - 2 * lax.rem(row, 2), 2 - hemi, 3 * (1 - hemi))

    def blk_peer(step):
        if near:
            return 2 * rows_near[step // 2] + (1 - side if step % 2 else side)
        return lax.rem(b + step, n_blk)

    def load(source, target, sem):
        copy = pltpu.make_async_copy(source, target, sem)
        copy.start()
        return copy

    def greet(sem):
        pl.semaphore_signal(sem, inc=1, device_id=(g, b + 1 - 2 * side), device_id_type=MESH)

        @pl.when(row > 0)
        def _():
            pl.semaphore_signal(sem, inc=1, device_id=(g, b - 2), device_id_type=MESH)

        @pl.when(row < last_row)
        def _():
            pl.semaphore_signal(sem, inc=1, device_id=(g, b + 2), device_id_type=MESH)

    greeters = 1 + jnp.minimum(row, 1) + jnp.minimum(last_row - row, 1)

    barrier = pltpu.get_barrier_semaphore()
    for step in range(1, n_grp):
        pl.semaphore_signal(barrier, inc=1, device_id=(grp_peer(step), b), device_id_type=MESH)
    if near:
        greet(barrier)
    else:
        for step in range(1, n_blk):
            pl.semaphore_signal(barrier, inc=1, device_id=(g, blk_peer(step)), device_id_type=MESH)

    first = [load(features, feat, in_sems.at[0]), load(col_scale, cscale, in_sems.at[1])]

    cols_load = load(cols_in, cols, in_sems.at[6])

    tile_loads = []
    for spot, step in enumerate(order):
        rows = pl.ds(blk_peer(step) * TPR, TPR)
        tile_loads.append(load(tiles.at[rows], held.at[rows], tile_sems.at[spot]))
    late = [
        load(row_scale, rscale, in_sems.at[2]),
        load(train_mask, mask, in_sems.at[3]),
        load(weight, wgt, in_sems.at[4]),
        load(cotangent, cot, in_sems.at[5]),
    ]

    if near:
        @pl.when((row > 0) & (row < last_row))
        def _():
            for step in (5, 7):
                arrived[blk_peer(step), CUT:] = jnp.zeros((feat.shape[0] - CUT, feat.shape[1]), BF16)

    for copy in first:
        copy.wait()
    sources[g] = (down_rows(cscale[...], feat.shape[1]) * feat[...].astype(F32)).astype(BF16)
    if near:
        pl.semaphore_wait(barrier, n_grp - 1 + greeters)
    else:
        pl.semaphore_wait(barrier, n_grp + n_blk - 2)

    src_copies = []
    for step in range(1, n_grp):
        copy = pltpu.make_async_remote_copy(
            src_ref=sources.at[g], dst_ref=sources.at[g],
            send_sem=src_send.at[step - 1], recv_sem=src_recv.at[step - 1],
            device_id=(grp_peer(step), b), device_id_type=MESH)
        copy.start()
        src_copies.append(copy)
    if near:
        greet(greet_sems.at[0])
        pl.semaphore_wait(greet_sems.at[0], greeters)
        pl.semaphore_signal(greet_sems.at[1], inc=1, device_id=(g, flip(b, 4)), device_id_type=MESH)
        pl.semaphore_wait(greet_sems.at[1], 1)
    cols_load.wait()
    for copy in tile_loads:
        copy.wait()
    for copy in src_copies:
        copy.wait_recv()

    def partial(block):
        base = block * TPR
        left = jnp.concatenate([held[base + k] for k in range(TPR)], axis=1)
        right = jnp.concatenate([sources[cols[base + k]] for k in range(TPR)], axis=0)
        return jnp.dot(left, right, preferred_element_type=F32)

    part_copies = []

    def pass_on(spot, rows, target, slot, sem, to):
        copy = pltpu.make_async_remote_copy(
            src_ref=outgoing.at[spot, rows], dst_ref=target, send_sem=part_send.at[slot],
            recv_sem=sem, device_id=(g, to), device_id_type=MESH)
        copy.start()
        part_copies.append(copy)

    tile = feat.shape[0]
    every, upper, lower = pl.ds(0, tile), pl.ds(0, CUT), pl.ds(CUT, tile - CUT)
    twin = b + 1 - 2 * side
    crossed, straight = order.index(5), order.index(4)
    middle = (row > 0) & (row < last_row)
    if near:
        outgoing[crossed] = partial(blk_peer(5)).astype(BF16)
        pass_on(crossed, lower, handed, n_blk - 1, hand_sem.at[0], twin)
    for spot, step in enumerate(order[:-1]):
        block = blk_peer(step)
        rows = upper if near and spot in (crossed, straight) else every
        if near and spot == straight:
            part = partial(block)
            outgoing[spot, :CUT] = part[:CUT].astype(BF16)
            kept[...] = part[CUT:]
        elif not near or spot != crossed:
            outgoing[spot] = partial(block).astype(BF16)
        pass_on(spot, rows, arrived.at[b, rows], spot, part_recv.at[b], block)
    mine[...] = partial(b)
    if near:
        pltpu.make_async_copy(handed, handed, hand_sem.at[0]).wait()
        outgoing[straight, CUT:] = (kept[...] + handed[...].astype(F32)).astype(BF16)
        pass_on(straight, lower, arrived.at[b, lower], n_blk, part_recv.at[b], blk_peer(4))

    for copy in late:
        copy.wait()
    row_full = down_rows(rscale[...], feat.shape[1])
    mask_full = down_rows(mask[...].astype(F32), cot.shape[1] // 2)
    masked = cot[...].astype(F32) * jnp.concatenate([mask_full, mask_full], axis=1)

    total = mine[...]
    for step in reversed(order[:-1]):
        block = blk_peer(step)
        slot, short = arrived.at[block], arrived.at[block, upper]

        def whole_slot(slot=slot, block=block):
            pltpu.make_async_copy(slot, slot, part_recv.at[block]).wait()

        if near and step in (5, 7):
            pl.when(jnp.logical_not(middle))(whole_slot)

            @pl.when(middle)
            def _(short=short, block=block):
                pltpu.make_async_copy(short, short, part_recv.at[block]).wait()
        else:
            whole_slot()
        total = total + slot[...].astype(F32)
    mixed = row_full * total

    high, low = split(mixed)
    w = wgt[...]
    pre = jnp.dot(jnp.concatenate([high, low], axis=1), jnp.concatenate([w, w], axis=0),
                  preferred_element_type=F32)
    square = pre * pre
    bent = jnp.tanh(ROOT * pre * (1.0 + CUBE * square))
    half = 0.5 * (1.0 + bent)
    hidden = (pre * half).astype(packed.dtype)
    for piece in range(top):
        packed[piece] = hidden[piece * 8:piece * 8 + 8]
    slope = half + 0.5 * pre * (1.0 - bent * bent) * (ROOT * (1.0 + 3.0 * CUBE * square))
    delta = slope * masked

    high_t, low_t = split(mixed.T)
    d_high, d_low = split(delta)
    grad = jnp.dot(jnp.concatenate([high_t, low_t, high_t], axis=1),
                   jnp.concatenate([d_high, d_high, d_low], axis=0), preferred_element_type=F32)
    if not pieces:
        for piece in range(grad.shape[0] // 8):
            packed[top + piece] = grad[piece * 8:piece * 8 + 8]
        for copy in src_copies + part_copies:
            copy.wait_send()
        return

    n = n_grp * n_blk
    me = g * n_blk + b
    span, first_blk = n_blk // 2, n_blk // 4
    owners = n_grp * span
    owner = (b >= first_blk) & (b < first_blk + span)
    seat = g * span + (b - first_blk)
    for piece in range(owners):
        grad_parts[piece] = grad[piece * 8:piece * 8 + 8].astype(GRAD_LINK)

    for mid in (1 - hemi, hemi):
        for turn in reversed(range(2 * n_grp)):
            to_g, to_b = flip(g, turn % n_grp), 2 * (mid + 1) + lax.rem(side + turn // n_grp, 2)
            to = to_g * span + (to_b - first_blk)

            def scatter(to=to, to_g=to_g, to_b=to_b):
                pltpu.make_async_remote_copy(
                    src_ref=grad_parts.at[to], dst_ref=grad_in.at[me],
                    send_sem=grad_sems.at[0], recv_sem=grad_sems.at[1],
                    device_id=(to_g, to_b), device_id_type=MESH).start()

            if turn == 0:
                pl.when(to_b != b)(scatter)
            else:
                scatter()
    some = grad_parts.at[pl.ds(0, owners - 1)]

    @pl.when(owner)
    def _():
        grad_in[me] = grad_parts[seat]
        others = grad_in.at[pl.ds(0, n - 1)]
        pltpu.make_async_copy(others, others, grad_sems.at[1]).wait()
        packed[top + seat] = jnp.sum(grad_in[...].astype(F32), axis=0).astype(GRAD_LINK)
        for turn in GATHER:
            pltpu.make_async_remote_copy(
                src_ref=packed.at[top + seat], dst_ref=packed.at[top + seat],
                send_sem=grad_sems.at[2], recv_sem=grad_sems.at[3],
                device_id=(flip(g, turn % n_grp), flip(b, turn // n_grp)), device_id_type=MESH).start()
        pltpu.make_async_copy(some, some, grad_sems.at[3]).wait()
        pltpu.make_async_copy(some, some, grad_sems.at[0]).wait()
        pltpu.make_async_copy(others, others, grad_sems.at[2]).wait()

    @pl.when(jnp.logical_not(owner))
    def _():
        pltpu.make_async_copy(grad_parts, grad_parts, grad_sems.at[3]).wait()
        pltpu.make_async_copy(grad_parts, grad_parts, grad_sems.at[0]).wait()

    for copy in src_copies + part_copies:
        copy.wait_send()


def shards(n_grp, n_blk, features, col_scale, row_scale, tiles, tile_cols, weight, cotangent, train_mask):
    nodes, fin = features.shape
    hid_width = weight.shape[1]
    tile = tiles.shape[1]
    n = n_grp * n_blk
    pieces = n_grp * (n_blk // 2) * 8 == fin
    hbm = pl.BlockSpec(memory_space=pltpu.HBM)
    if pieces:
        spare, landing = (fin // 8, 8, hid_width), (n, 8, hid_width)
    else:
        spare = landing = (1, 8, 128)
    out_type = BF16 if pieces else F32
    hbm = pl.BlockSpec(memory_space=pltpu.HBM)
    if pieces:
        spare, landing = (fin // 8, 8, hid_width), (n, 8, hid_width)
    else:
        spare = landing = (1, 8, 128)
    grad_type = GRAD_LINK if pieces else F32
    grad_shape = jax.ShapeDtypeStruct((fin, hid_width), grad_type)
    dma = pltpu.SemaphoreType.DMA
    packed = pl.pallas_call(
        functools.partial(kernel, n_grp, n_blk, pieces),
        out_shape=pltpu.VMEM(((nodes + fin) // 8, 8, hid_width), out_type),
        in_specs=[hbm] * 8,
        out_specs=pl.BlockSpec(memory_space=pltpu.VMEM),
        scratch_shapes=[
            pltpu.SMEM(tile_cols.shape, jnp.int32),
            pltpu.VMEM((nodes, fin), BF16),
            pltpu.VMEM((1, nodes), F32),
            pltpu.VMEM((1, nodes), F32),
            pltpu.VMEM((1, nodes), jnp.int32),
            pltpu.VMEM((fin, hid_width), BF16),
            pltpu.VMEM((nodes, hid_width), BF16),
            pltpu.VMEM(tiles.shape, BF16),
            pltpu.VMEM((n_grp, tile, fin), BF16),
            pltpu.VMEM((tile, fin), F32),
            pltpu.VMEM((n_blk - 1, tile, fin), BF16),
            pltpu.VMEM((n_blk, tile, fin), BF16),
            pltpu.VMEM(spare, GRAD_LINK),
            pltpu.VMEM(landing, GRAD_LINK),
            dma((7,)), dma((n_blk,)), dma((n_grp - 1,)), dma((n_grp - 1,)),
            dma((n_blk + 1,)), dma((n_blk,)), dma((4,)),
            pltpu.SemaphoreType.REGULAR((2,)),
            pltpu.VMEM((tile - CUT, fin), BF16), pltpu.VMEM((tile - CUT, fin), F32), dma((1,)),
        ],
        compiler_params=pltpu.CompilerParams(
            collective_id=0, has_side_effects=True, vmem_limit_bytes=VLIM),
    )(*[pltpu.with_memory_space_constraint(x, pltpu.HBM) for x in (
        tile_cols, features, col_scale.reshape(1, nodes), row_scale.reshape(1, nodes), tiles, weight,
        cotangent, train_mask.reshape(1, nodes))])
    hidden, grad = packed[:nodes // 8].reshape(nodes, hid_width).astype(BF16), packed[nodes // 8:].reshape(fin, hid_width).astype(F32)
    if not pieces:
        grad = lax.psum(grad, ("grp", "blk"))
    return hidden, grad


def solution(mesh):
    in_specs = (
        P(("grp", "blk"), None),
        P(("grp", "blk")),
        P(("grp", "blk")),
        P(("grp", "blk"), None, None),
        P(("grp", "blk")),
        P(),
        P(("grp", "blk"), None),
        P(("grp", "blk")),
    )
    out_specs = (P(("grp", "blk"), None), P())
    body = functools.partial(shards, mesh.shape["grp"], mesh.shape["blk"])
    return jax.shard_map(body, mesh=mesh, in_specs=in_specs, out_specs=out_specs, check_vma=False)
```

```python
import functools
import math

import jax
import jax.numpy as jnp
from jax import lax
from jax.experimental import pallas as pl
from jax.experimental.pallas import tpu as pltpu
from jax.sharding import PartitionSpec as P

TPR = 4
ROOT = math.sqrt(2.0 / math.pi)
CUBE = 0.044715
MESH = pl.DeviceIdType.MESH
F32 = jnp.float32
BF16 = jnp.bfloat16
GRAD_LINK = BF16
VLIM = 32 * 1024 * 1024
CUT = 48
ROWS = (0, 3, 2, 1)


def far_first(count):
    return sorted(range(1, count), key=lambda step: abs(2 * step - count))


def split(value):
    high = value.astype(BF16)
    return high, (value - high.astype(F32)).astype(BF16)


def down_rows(row, width):
    return jnp.broadcast_to(row, (width, row.shape[1])).T


def kernel(n_grp, n_blk, near, cols_in, features, col_scale, row_scale, tiles, weight, cotangent,
           train_mask, packed, cols, feat, cscale, rscale, mask, wgt, cot, held, sources,
           mine, outgoing, arrived, grad_parts, grad_in, grad_all, in_sems, tile_sems, src_send,
           src_recv, part_send, part_recv, grad_sems, greet_sems,
           handed, kept, hand_sem):
    deep, hid_width = grad_parts.shape[1], packed.shape[1]
    top = feat.shape[0]
    g, b = lax.axis_index("grp"), lax.axis_index("blk")
    last_row = n_blk // 2 - 1
    row, side = b // 2, lax.rem(b, 2)
    order = list(range(n_blk - 1, -1, -1)) if near else far_first(n_blk) + [0]

    def flip(index, mask):
        out, weight = 0, 1
        while weight <= mask:
            bit = lax.rem(index // weight, 2)
            out = out + weight * (1 - 2 * bit) * (mask // weight % 2)
            weight *= 2
        return index + out

    def grp_peer(step):
        return flip(g, step) if near else lax.rem(g + step, n_grp)

    hemi = row // 2
    rows_near = (row, row + 1 - 2 * lax.rem(row, 2), 2 - hemi, 3 * (1 - hemi))

    def blk_peer(step):
        if near:
            return 2 * rows_near[step // 2] + (1 - side if step % 2 else side)
        return lax.rem(b + step, n_blk)

    def load(source, target, sem):
        copy = pltpu.make_async_copy(source, target, sem)
        copy.start()
        return copy

    def greet(sem):
        pl.semaphore_signal(sem, inc=1, device_id=(g, b + 1 - 2 * side), device_id_type=MESH)

        @pl.when(row > 0)
        def _():
            pl.semaphore_signal(sem, inc=1, device_id=(g, b - 2), device_id_type=MESH)

        @pl.when(row < last_row)
        def _():
            pl.semaphore_signal(sem, inc=1, device_id=(g, b + 2), device_id_type=MESH)

    greeters = 1 + jnp.minimum(row, 1) + jnp.minimum(last_row - row, 1)

    barrier = pltpu.get_barrier_semaphore()
    for step in range(1, n_grp):
        pl.semaphore_signal(barrier, inc=1, device_id=(grp_peer(step), b), device_id_type=MESH)
    if near:
        greet(barrier)
    else:
        for step in range(1, n_blk):
            pl.semaphore_signal(barrier, inc=1, device_id=(g, blk_peer(step)), device_id_type=MESH)

    first = [load(features, feat, in_sems.at[0]), load(col_scale, cscale, in_sems.at[1])]

    cols_load = load(cols_in, cols, in_sems.at[6])

    tile_loads = []
    for spot, step in enumerate(order):
        rows = pl.ds(blk_peer(step) * TPR, TPR)
        tile_loads.append(load(tiles.at[rows], held.at[rows], tile_sems.at[spot]))
    late = [
        load(row_scale, rscale, in_sems.at[2]),
        load(train_mask, mask, in_sems.at[3]),
        load(weight, wgt, in_sems.at[4]),
        load(cotangent, cot, in_sems.at[5]),
    ]

    if near:
        @pl.when((row > 0) & (row < last_row))
        def _():
            for step in (5, 7):
                arrived[blk_peer(step), CUT:] = jnp.zeros((feat.shape[0] - CUT, feat.shape[1]), BF16)

    for copy in first:
        copy.wait()
    sources[g] = (down_rows(cscale[...], feat.shape[1]) * feat[...].astype(F32)).astype(BF16)
    if near:
        pl.semaphore_wait(barrier, n_grp - 1 + greeters)
    else:
        pl.semaphore_wait(barrier, n_grp + n_blk - 2)

    src_copies = []
    for step in range(1, n_grp):
        copy = pltpu.make_async_remote_copy(
            src_ref=sources.at[g], dst_ref=sources.at[g],
            send_sem=src_send.at[step - 1], recv_sem=src_recv.at[step - 1],
            device_id=(grp_peer(step), b), device_id_type=MESH)
        copy.start()
        src_copies.append(copy)
    if near:
        greet(greet_sems.at[0])
        pl.semaphore_wait(greet_sems.at[0], greeters)
        pl.semaphore_signal(greet_sems.at[1], inc=1, device_id=(g, flip(b, 4)), device_id_type=MESH)
        pl.semaphore_wait(greet_sems.at[1], 1)
    cols_load.wait()
    for copy in tile_loads:
        copy.wait()
    for copy in src_copies:
        copy.wait_recv()

    def partial(block):
        base = block * TPR
        left = jnp.concatenate([held[base + k] for k in range(TPR)], axis=1)
        right = jnp.concatenate([sources[cols[base + k]] for k in range(TPR)], axis=0)
        return jnp.dot(left, right, preferred_element_type=F32)

    part_copies = []

    def pass_on(spot, rows, target, slot, sem, to):
        copy = pltpu.make_async_remote_copy(
            src_ref=outgoing.at[spot, rows], dst_ref=target, send_sem=part_send.at[slot],
            recv_sem=sem, device_id=(g, to), device_id_type=MESH)
        copy.start()
        part_copies.append(copy)

    tile = feat.shape[0]
    every, upper, lower = pl.ds(0, tile), pl.ds(0, CUT), pl.ds(CUT, tile - CUT)
    twin = b + 1 - 2 * side
    crossed, straight = order.index(5), order.index(4)
    middle = (row > 0) & (row < last_row)
    if near:
        outgoing[crossed] = partial(blk_peer(5)).astype(BF16)
        pass_on(crossed, lower, handed, n_blk - 1, hand_sem.at[0], twin)
    for spot, step in enumerate(order[:-1]):
        block = blk_peer(step)
        rows = upper if near and spot in (crossed, straight) else every
        if near and spot == straight:
            part = partial(block)
            outgoing[spot, :CUT] = part[:CUT].astype(BF16)
            kept[...] = part[CUT:]
        elif not near or spot != crossed:
            outgoing[spot] = partial(block).astype(BF16)
        pass_on(spot, rows, arrived.at[b, rows], spot, part_recv.at[b], block)
    mine[...] = partial(b)
    if near:
        pltpu.make_async_copy(handed, handed, hand_sem.at[0]).wait()
        outgoing[straight, CUT:] = (kept[...] + handed[...].astype(F32)).astype(BF16)
        pass_on(straight, lower, arrived.at[b, lower], n_blk, part_recv.at[b], blk_peer(4))

    for copy in late:
        copy.wait()
    row_full = down_rows(rscale[...], feat.shape[1])
    mask_full = down_rows(mask[...].astype(F32), cot.shape[1] // 2)
    masked = cot[...].astype(F32) * jnp.concatenate([mask_full, mask_full], axis=1)

    total = mine[...]
    for step in (1, 2, 3, 5, 7, 6, 4) if near else reversed(order[:-1]):
        block = blk_peer(step)
        slot, short = arrived.at[block], arrived.at[block, upper]

        def whole_slot(slot=slot, block=block):
            pltpu.make_async_copy(slot, slot, part_recv.at[block]).wait()

        if near and step in (5, 7):
            pl.when(jnp.logical_not(middle))(whole_slot)

            @pl.when(middle)
            def _(short=short, block=block):
                pltpu.make_async_copy(short, short, part_recv.at[block]).wait()
        else:
            whole_slot()
        total = total + slot[...].astype(F32)
    mixed = row_full * total

    high, low = split(mixed)
    w = wgt[...]
    pre = jnp.dot(jnp.concatenate([high, low], axis=1), jnp.concatenate([w, w], axis=0),
                  preferred_element_type=F32)
    square = pre * pre
    bent = jnp.tanh(ROOT * pre * (1.0 + CUBE * square))
    half = 0.5 * (1.0 + bent)
    hidden = (pre * half).astype(BF16).astype(packed.dtype)
    packed[:top] = -hidden
    slope = half + 0.5 * pre * (1.0 - bent * bent) * (ROOT * (1.0 + 3.0 * CUBE * square))
    delta = slope * masked

    high_t, low_t = split(mixed.T)
    d_high, d_low = split(delta)
    grad = jnp.dot(jnp.concatenate([high_t, low_t, high_t], axis=1),
                   jnp.concatenate([d_high, d_high, d_low], axis=0), preferred_element_type=F32)
    if not near:
        packed[top:] = grad
        for copy in src_copies + part_copies:
            copy.wait_send()
        return

    span = n_blk // 4
    owners = n_grp * span
    senders = 2 * owners
    owner = row == 1 + hemi
    seat = g * span + side
    spot_in = g * 2 * span + b - 2 * span * hemi
    for piece in range(owners):
        grad_parts[piece] = grad[piece * deep:piece * deep + deep].astype(GRAD_LINK)

    for turn in reversed(range(owners)):
        to_g, to_side = flip(g, turn % n_grp), lax.rem(side + turn // n_grp, 2)

        def scatter(to_g=to_g, to_side=to_side):
            pltpu.make_async_remote_copy(
                src_ref=grad_parts.at[to_g * span + to_side], dst_ref=grad_in.at[spot_in],
                send_sem=grad_sems.at[0], recv_sem=grad_sems.at[1],
                device_id=(to_g, 2 * (1 + hemi) + to_side), device_id_type=MESH).start()

        if turn == 0:
            pl.when(jnp.logical_not(owner))(scatter)
        else:
            scatter()
    for copy in src_copies + part_copies:
        copy.wait_send()

    @pl.when(owner)
    def _():
        grad_in[spot_in] = grad_parts[seat]
        others, some = grad_in.at[pl.ds(0, senders - 1)], grad_parts.at[pl.ds(0, owners - 1)]
        pltpu.make_async_copy(others, others, grad_sems.at[1]).wait()
        own = owners * hemi + seat
        grad_all[own] = jnp.sum(grad_in[...].astype(F32), axis=0).astype(GRAD_LINK)
        for row_to in ROWS:
            for turn in range(2 * n_grp):
                to_g, to_b = turn % n_grp, 2 * row_to + turn // n_grp

                def gather(to_g=to_g, to_b=to_b):
                    pltpu.make_async_remote_copy(
                        src_ref=grad_all.at[own], dst_ref=grad_all.at[own],
                        send_sem=grad_sems.at[2], recv_sem=grad_sems.at[3],
                        device_id=(to_g, to_b), device_id_type=MESH).start()

                if row_to in (1, 2):
                    pl.when((to_g != g) | (to_b != b))(gather)
                else:
                    gather()
        pltpu.make_async_copy(some, some, grad_sems.at[0]).wait()
        rest = grad_all.at[pl.ds(0, 2 * owners - 1)]
        pltpu.make_async_copy(rest, rest, grad_sems.at[3]).wait()
        sent = held.at[pl.ds(0, n_grp * n_blk - 1), pl.ds(0, deep * hid_width // held.shape[2])]
        pltpu.make_async_copy(sent, sent, grad_sems.at[2]).wait()

    @pl.when(jnp.logical_not(owner))
    def _():
        pltpu.make_async_copy(grad_parts, grad_parts, grad_sems.at[0]).wait()
        pltpu.make_async_copy(grad_all, grad_all, grad_sems.at[3]).wait()

    for piece in range(owners):
        packed[top + piece * deep:top + piece * deep + deep] = grad_all[piece].astype(F32) + grad_all[owners + piece].astype(F32)


def shards(n_grp, n_blk, features, col_scale, row_scale, tiles, tile_cols, weight, cotangent, train_mask):
    nodes, fin = features.shape
    hid_width = weight.shape[1]
    tile = tiles.shape[1]
    near = n_grp == 4 and n_blk == 8 and fin == 128
    deep = 16 if near else 8
    hbm = pl.BlockSpec(memory_space=pltpu.HBM)
    spare = (fin // deep, deep, hid_width) if near else (1, deep, 128)
    landing = (2 * fin // deep, deep, hid_width) if near else (1, deep, 128)
    dma = pltpu.SemaphoreType.DMA
    packed = pl.pallas_call(
        functools.partial(kernel, n_grp, n_blk, near),
        out_shape=pltpu.VMEM((nodes + fin, hid_width), F32),
        in_specs=[hbm] * 8,
        out_specs=pl.BlockSpec(memory_space=pltpu.VMEM),
        scratch_shapes=[
            pltpu.SMEM(tile_cols.shape, jnp.int32),
            pltpu.VMEM((nodes, fin), BF16),
            pltpu.VMEM((1, nodes), F32),
            pltpu.VMEM((1, nodes), F32),
            pltpu.VMEM((1, nodes), jnp.int32),
            pltpu.VMEM((fin, hid_width), BF16),
            pltpu.VMEM((nodes, hid_width), BF16),
            pltpu.VMEM(tiles.shape, BF16),
            pltpu.VMEM((n_grp, tile, fin), BF16),
            pltpu.VMEM((tile, fin), F32),
            pltpu.VMEM((n_blk - 1, tile, fin), BF16),
            pltpu.VMEM((n_blk, tile, fin), BF16),
            pltpu.VMEM(spare, GRAD_LINK),
            pltpu.VMEM(landing, GRAD_LINK),
            pltpu.VMEM(landing, GRAD_LINK),
            dma((7,)), dma((n_blk,)), dma((n_grp - 1,)), dma((n_grp - 1,)),
            dma((n_blk + 1,)), dma((n_blk,)), dma((4,)),
            pltpu.SemaphoreType.REGULAR((2,)),
            pltpu.VMEM((tile - CUT, fin), BF16), pltpu.VMEM((tile - CUT, fin), F32), dma((1,)),
        ],
        compiler_params=pltpu.CompilerParams(
            collective_id=0, has_side_effects=True, vmem_limit_bytes=VLIM),
    )(*[pltpu.with_memory_space_constraint(x, pltpu.HBM) for x in (
        tile_cols, features, col_scale.reshape(1, nodes), row_scale.reshape(1, nodes), tiles, weight,
        cotangent, train_mask.reshape(1, nodes))])
    hidden, grad = (-packed[:nodes]).astype(BF16), packed[nodes:]
    if not near:
        grad = lax.psum(grad, ("grp", "blk"))
    return hidden, grad


def solution(mesh):
    in_specs = (
        P(("grp", "blk"), None),
        P(("grp", "blk")),
        P(("grp", "blk")),
        P(("grp", "blk"), None, None),
        P(("grp", "blk")),
        P(),
        P(("grp", "blk"), None),
        P(("grp", "blk")),
    )
    out_specs = (P(("grp", "blk"), None), P())
    body = functools.partial(shards, mesh.shape["grp"], mesh.shape["blk"])
    return jax.shard_map(body, mesh=mesh, in_specs=in_specs, out_specs=out_specs, check_vma=False)
```

```python
import functools
import math

import jax
import jax.numpy as jnp
from jax import lax
from jax.experimental import pallas as pl
from jax.experimental.pallas import tpu as pltpu
from jax.sharding import PartitionSpec as P

TPR = 4
ROOT = math.sqrt(2.0 / math.pi)
CUBE = 0.044715
MESH = pl.DeviceIdType.MESH
F32 = jnp.float32
BF16 = jnp.bfloat16
VLIM = 32 * 1024 * 1024
CUT = 48
ROWS = (0, 3, 2, 1)


def far_first(count):
    return sorted(range(1, count), key=lambda step: abs(2 * step - count))


def split(value):
    high = value.astype(BF16)
    return high, (value - high.astype(F32)).astype(BF16)


def down_rows(row, width):
    return jnp.broadcast_to(row, (width, row.shape[1])).T


def kernel(n_grp, n_blk, near, cols_in, features, col_scale, row_scale, tiles, weight, cotangent,
           train_mask, packed, cols, feat, cscale, rscale, mask, wgt, cot, held, sources,
           mine, outgoing, arrived, grad_parts, grad_in, in_sems, tile_sems, src_send,
           src_recv, part_send, part_recv, grad_sems, greet_sems,
           handed, kept, hand_sem):
    deep, hid_width = grad_parts.shape[1], packed.shape[1]
    top = feat.shape[0]
    g, b = lax.axis_index("grp"), lax.axis_index("blk")
    last_row = n_blk // 2 - 1
    row, side = b // 2, lax.rem(b, 2)
    order = list(range(n_blk - 1, -1, -1)) if near else far_first(n_blk) + [0]

    def flip(index, mask):
        out, weight = 0, 1
        while weight <= mask:
            bit = lax.rem(index // weight, 2)
            out = out + weight * (1 - 2 * bit) * (mask // weight % 2)
            weight *= 2
        return index + out

    def grp_peer(step):
        return flip(g, step) if near else lax.rem(g + step, n_grp)

    hemi = row // 2
    rows_near = (row, row + 1 - 2 * lax.rem(row, 2), 2 - hemi, 3 * (1 - hemi))

    def blk_peer(step):
        if near:
            return 2 * rows_near[step // 2] + (1 - side if step % 2 else side)
        return lax.rem(b + step, n_blk)

    def load(source, target, sem):
        copy = pltpu.make_async_copy(source, target, sem)
        copy.start()
        return copy

    def greet(sem):
        pl.semaphore_signal(sem, inc=1, device_id=(g, b + 1 - 2 * side), device_id_type=MESH)

        @pl.when(row > 0)
        def _():
            pl.semaphore_signal(sem, inc=1, device_id=(g, b - 2), device_id_type=MESH)

        @pl.when(row < last_row)
        def _():
            pl.semaphore_signal(sem, inc=1, device_id=(g, b + 2), device_id_type=MESH)

    greeters = 1 + jnp.minimum(row, 1) + jnp.minimum(last_row - row, 1)

    barrier = pltpu.get_barrier_semaphore()
    for step in range(1, n_grp):
        pl.semaphore_signal(barrier, inc=1, device_id=(grp_peer(step), b), device_id_type=MESH)
    if near:
        greet(barrier)
    else:
        for step in range(1, n_blk):
            pl.semaphore_signal(barrier, inc=1, device_id=(g, blk_peer(step)), device_id_type=MESH)

    first = [load(features, feat, in_sems.at[0]), load(col_scale, cscale, in_sems.at[1])]

    cols_load = load(cols_in, cols, in_sems.at[6])

    tile_loads = []
    for spot, step in enumerate(order):
        rows = pl.ds(blk_peer(step) * TPR, TPR)
        tile_loads.append(load(tiles.at[rows], held.at[rows], tile_sems.at[spot]))
    late = [
        load(row_scale, rscale, in_sems.at[2]),
        load(train_mask, mask, in_sems.at[3]),
        load(weight, wgt, in_sems.at[4]),
        load(cotangent, cot, in_sems.at[5]),
    ]

    if near:
        @pl.when((row > 0) & (row < last_row))
        def _():
            for step in (5, 7):
                arrived[blk_peer(step), CUT:] = jnp.zeros((feat.shape[0] - CUT, feat.shape[1]), BF16)

    for copy in first:
        copy.wait()
    sources[g] = (down_rows(cscale[...], feat.shape[1]) * feat[...].astype(F32)).astype(BF16)
    if near:
        pl.semaphore_wait(barrier, n_grp - 1 + greeters)
    else:
        pl.semaphore_wait(barrier, n_grp + n_blk - 2)

    src_copies = []
    for step in range(1, n_grp):
        copy = pltpu.make_async_remote_copy(
            src_ref=sources.at[g], dst_ref=sources.at[g],
            send_sem=src_send.at[step - 1], recv_sem=src_recv.at[step - 1],
            device_id=(grp_peer(step), b), device_id_type=MESH)
        copy.start()
        src_copies.append(copy)
    if near:
        greet(greet_sems.at[0])
        pl.semaphore_wait(greet_sems.at[0], greeters)
        pl.semaphore_signal(greet_sems.at[1], inc=1, device_id=(g, flip(b, 4)), device_id_type=MESH)
        pl.semaphore_wait(greet_sems.at[1], 1)
    cols_load.wait()
    for copy in tile_loads:
        copy.wait()
    for copy in src_copies:
        copy.wait_recv()

    def partial(block):
        base = block * TPR
        left = jnp.concatenate([held[base + k] for k in range(TPR)], axis=1)
        right = jnp.concatenate([sources[cols[base + k]] for k in range(TPR)], axis=0)
        return jnp.dot(left, right, preferred_element_type=F32)

    part_copies = []

    def pass_on(spot, rows, target, slot, sem, to):
        copy = pltpu.make_async_remote_copy(
            src_ref=outgoing.at[spot, rows], dst_ref=target, send_sem=part_send.at[slot],
            recv_sem=sem, device_id=(g, to), device_id_type=MESH)
        copy.start()
        part_copies.append(copy)

    tile = feat.shape[0]
    every, upper, lower = pl.ds(0, tile), pl.ds(0, CUT), pl.ds(CUT, tile - CUT)
    twin = b + 1 - 2 * side
    crossed, straight = order.index(5), order.index(4)
    middle = (row > 0) & (row < last_row)
    if near:
        outgoing[crossed] = partial(blk_peer(5)).astype(BF16)
        pass_on(crossed, lower, handed, n_blk - 1, hand_sem.at[0], twin)
    for spot, step in enumerate(order[:-1]):
        block = blk_peer(step)
        rows = upper if near and spot in (crossed, straight) else every
        if near and spot == straight:
            part = partial(block)
            outgoing[spot, :CUT] = part[:CUT].astype(BF16)
            kept[...] = part[CUT:]
        elif not near or spot != crossed:
            outgoing[spot] = partial(block).astype(BF16)
        pass_on(spot, rows, arrived.at[b, rows], spot, part_recv.at[b], block)
    mine[...] = partial(b)
    if near:
        pltpu.make_async_copy(handed, handed, hand_sem.at[0]).wait()
        outgoing[straight, CUT:] = (kept[...] + handed[...].astype(F32)).astype(BF16)
        pass_on(straight, lower, arrived.at[b, lower], n_blk, part_recv.at[b], blk_peer(4))

    for copy in late:
        copy.wait()
    row_full = down_rows(rscale[...], feat.shape[1])
    mask_full = down_rows(mask[...].astype(F32), cot.shape[1] // 2)
    masked = cot[...].astype(F32) * jnp.concatenate([mask_full, mask_full], axis=1)

    total = mine[...]
    for step in (1, 2, 3, 5, 7, 6, 4) if near else reversed(order[:-1]):
        block = blk_peer(step)
        slot, short = arrived.at[block], arrived.at[block, upper]

        def whole_slot(slot=slot, block=block):
            pltpu.make_async_copy(slot, slot, part_recv.at[block]).wait()

        if near and step in (5, 7):
            pl.when(jnp.logical_not(middle))(whole_slot)

            @pl.when(middle)
            def _(short=short, block=block):
                pltpu.make_async_copy(short, short, part_recv.at[block]).wait()
        else:
            whole_slot()
        total = total + slot[...].astype(F32)
    mixed = row_full * total

    high, low = split(mixed)
    w = wgt[...]
    pre = jnp.dot(jnp.concatenate([high, low], axis=1), jnp.concatenate([w, w], axis=0),
                  preferred_element_type=F32)
    square = pre * pre
    bent = jnp.tanh(ROOT * pre * (1.0 + CUBE * square))
    half = 0.5 * (1.0 + bent)
    hidden = (pre * half).astype(BF16).astype(packed.dtype)
    slope = half + 0.5 * pre * (1.0 - bent * bent) * (ROOT * (1.0 + 3.0 * CUBE * square))
    delta = slope * masked

    high_t, low_t = split(mixed.T)
    d_high, d_low = split(delta)
    grad = jnp.dot(jnp.concatenate([high_t, low_t, high_t], axis=1),
                   jnp.concatenate([d_high, d_high, d_low], axis=0), preferred_element_type=F32)
    if not near:
        packed[:top] = hidden
        packed[top:] = grad
        for copy in src_copies + part_copies:
            copy.wait_send()
        return

    owners, senders = grad_parts.shape[0], grad_in.shape[0]
    floor, core = g // 2, lax.rem(g, 2)
    owner = (row > 0) & (row < last_row) & (core == 1)
    me = g * n_blk + b
    for piece in range(owners):
        grad_parts[piece] = grad[piece * deep:piece * deep + deep].astype(BF16)

    for mid in (1 - hemi, hemi):
        for turn in reversed(range(4)):
            to_floor, to_side = lax.rem(floor + turn // 2, 2), lax.rem(side + turn, 2)
            to_g, to_b = 2 * to_floor + 1, 2 * (1 + mid) + to_side

            def scatter(to_g=to_g, to_b=to_b, to_seat=4 * mid + 2 * to_floor + to_side):
                pltpu.make_async_remote_copy(
                    src_ref=grad_parts.at[to_seat], dst_ref=grad_in.at[me],
                    send_sem=grad_sems.at[0], recv_sem=grad_sems.at[1],
                    device_id=(to_g, to_b), device_id_type=MESH).start()

            if turn == 0:
                pl.when((to_g != g) | (to_b != b))(scatter)
            else:
                scatter()
    packed[:top] = hidden
    for copy in src_copies + part_copies:
        copy.wait_send()
    gradient = packed.at[pl.ds(top, owners * deep)]

    @pl.when(owner)
    def _():
        seat = 4 * hemi + 2 * floor + side
        grad_in[me] = grad_parts[seat]
        others, some = grad_in.at[pl.ds(0, senders - 1)], grad_parts.at[pl.ds(0, owners - 1)]
        pltpu.make_async_copy(others, others, grad_sems.at[1]).wait()
        own = pl.ds(pl.multiple_of(top + seat * deep, deep), deep)
        packed[own] = jnp.sum(grad_in[...].astype(F32), axis=0).astype(BF16)
        for row_to in ROWS:
            for turn in range(2 * n_grp):
                to_g, to_b = turn % n_grp, 2 * row_to + turn // n_grp

                def gather(to_g=to_g, to_b=to_b):
                    pltpu.make_async_remote_copy(
                        src_ref=packed.at[own], dst_ref=packed.at[own],
                        send_sem=grad_sems.at[2], recv_sem=grad_sems.at[3],
                        device_id=(to_g, to_b), device_id_type=MESH).start()

                if row_to in (1, 2) and to_g % 2:
                    pl.when((to_g != g) | (to_b != b))(gather)
                else:
                    gather()
        pltpu.make_async_copy(some, some, grad_sems.at[0]).wait()
        rest = packed.at[pl.ds(top, (owners - 1) * deep)]
        pltpu.make_async_copy(rest, rest, grad_sems.at[3]).wait()
        pltpu.make_async_copy(others, others, grad_sems.at[2]).wait()

    @pl.when(jnp.logical_not(owner))
    def _():
        pltpu.make_async_copy(grad_parts, grad_parts, grad_sems.at[0]).wait()
        pltpu.make_async_copy(gradient, gradient, grad_sems.at[3]).wait()


def shards(n_grp, n_blk, features, col_scale, row_scale, tiles, tile_cols, weight, cotangent, train_mask):
    nodes, fin = features.shape
    hid_width = weight.shape[1]
    tile = tiles.shape[1]
    near = n_grp == 4 and n_blk == 8 and fin == 128
    hbm = pl.BlockSpec(memory_space=pltpu.HBM)
    deep = 16 if near else 8
    spare = (fin // deep if near else 1, deep, hid_width)
    landing = (n_grp * n_blk if near else 1, deep, hid_width)
    out_type = BF16 if near else F32
    dma = pltpu.SemaphoreType.DMA
    packed = pl.pallas_call(
        functools.partial(kernel, n_grp, n_blk, near),
        out_shape=pltpu.VMEM((nodes + fin, hid_width), out_type),
        in_specs=[hbm] * 8,
        out_specs=pl.BlockSpec(memory_space=pltpu.VMEM),
        scratch_shapes=[
            pltpu.SMEM(tile_cols.shape, jnp.int32),
            pltpu.VMEM((nodes, fin), BF16),
            pltpu.VMEM((1, nodes), F32),
            pltpu.VMEM((1, nodes), F32),
            pltpu.VMEM((1, nodes), jnp.int32),
            pltpu.VMEM((fin, hid_width), BF16),
            pltpu.VMEM((nodes, hid_width), BF16),
            pltpu.VMEM(tiles.shape, BF16),
            pltpu.VMEM((n_grp, tile, fin), BF16),
            pltpu.VMEM((tile, fin), F32),
            pltpu.VMEM((n_blk - 1, tile, fin), BF16),
            pltpu.VMEM((n_blk, tile, fin), BF16),
            pltpu.VMEM(spare, BF16),
            pltpu.VMEM(landing, BF16),
            dma((7,)), dma((n_blk,)), dma((n_grp - 1,)), dma((n_grp - 1,)),
            dma((n_blk + 1,)), dma((n_blk,)), dma((4,)),
            pltpu.SemaphoreType.REGULAR((2,)),
            pltpu.VMEM((tile - CUT, fin), BF16), pltpu.VMEM((tile - CUT, fin), F32), dma((1,)),
        ],
        compiler_params=pltpu.CompilerParams(
            collective_id=0, has_side_effects=True, vmem_limit_bytes=VLIM),
    )(*[pltpu.with_memory_space_constraint(x, pltpu.HBM) for x in (
        tile_cols, features, col_scale.reshape(1, nodes), row_scale.reshape(1, nodes), tiles, weight,
        cotangent, train_mask.reshape(1, nodes))])
    hidden, grad = packed[:nodes].astype(BF16), packed[nodes:].astype(F32)
    if not near:
        grad = lax.psum(grad, ("grp", "blk"))
    return hidden, grad


def solution(mesh):
    in_specs = (
        P(("grp", "blk"), None),
        P(("grp", "blk")),
        P(("grp", "blk")),
        P(("grp", "blk"), None, None),
        P(("grp", "blk")),
        P(),
        P(("grp", "blk"), None),
        P(("grp", "blk")),
    )
    out_specs = (P(("grp", "blk"), None), P())
    body = functools.partial(shards, mesh.shape["grp"], mesh.shape["blk"])
    return jax.shard_map(body, mesh=mesh, in_specs=in_specs, out_specs=out_specs, check_vma=False)
```

```python
import functools
import math

import jax
import jax.numpy as jnp
from jax import lax
from jax.experimental import pallas as pl
from jax.experimental.pallas import tpu as pltpu
from jax.sharding import PartitionSpec as P

TPR = 4
ROOT = math.sqrt(2.0 / math.pi)
CUBE = 0.044715
MESH = pl.DeviceIdType.MESH
F32 = jnp.float32
BF16 = jnp.bfloat16
VLIM = 32 * 1024 * 1024
CUTS = (48, 16)
ROWS = (0, 3, 2, 1)


def far_first(count):
    return sorted(range(1, count), key=lambda step: abs(2 * step - count))


def split(value):
    high = value.astype(BF16)
    return high, (value - high.astype(F32)).astype(BF16)


def down_rows(row, width):
    return jnp.broadcast_to(row, (width, row.shape[1])).T


def kernel(n_grp, n_blk, near, cols_in, features, col_scale, row_scale, tiles, weight, cotangent,
           train_mask, packed, cols, feat, cscale, rscale, mask, wgt, cot, held, sources,
           mine, outgoing, arrived, grad_parts, grad_in, in_sems, tile_sems, src_send,
           src_recv, part_send, part_recv, grad_sems, greet_sems,
           handed, kept, hand_sem):
    deep, hid_width = grad_parts.shape[1], packed.shape[1]
    top = feat.shape[0]
    g, b = lax.axis_index("grp"), lax.axis_index("blk")
    last_row = n_blk // 2 - 1
    row, side = b // 2, lax.rem(b, 2)
    order = list(range(n_blk - 1, -1, -1)) if near else far_first(n_blk) + [0]

    def flip(index, mask):
        out, weight = 0, 1
        while weight <= mask:
            bit = lax.rem(index // weight, 2)
            out = out + weight * (1 - 2 * bit) * (mask // weight % 2)
            weight *= 2
        return index + out

    def grp_peer(step):
        return flip(g, step) if near else lax.rem(g + step, n_grp)

    hemi = row // 2
    rows_near = (row, row + 1 - 2 * lax.rem(row, 2), 2 - hemi, 3 * (1 - hemi))

    def blk_peer(step):
        if near:
            return 2 * rows_near[step // 2] + (1 - side if step % 2 else side)
        return lax.rem(b + step, n_blk)

    def load(source, target, sem):
        copy = pltpu.make_async_copy(source, target, sem)
        copy.start()
        return copy

    def greet(sem):
        pl.semaphore_signal(sem, inc=1, device_id=(g, b + 1 - 2 * side), device_id_type=MESH)

        @pl.when(row > 0)
        def _():
            pl.semaphore_signal(sem, inc=1, device_id=(g, b - 2), device_id_type=MESH)

        @pl.when(row < last_row)
        def _():
            pl.semaphore_signal(sem, inc=1, device_id=(g, b + 2), device_id_type=MESH)

    greeters = 1 + jnp.minimum(row, 1) + jnp.minimum(last_row - row, 1)

    barrier = pltpu.get_barrier_semaphore()
    for step in range(1, n_grp):
        pl.semaphore_signal(barrier, inc=1, device_id=(grp_peer(step), b), device_id_type=MESH)
    if near:
        greet(barrier)
    else:
        for step in range(1, n_blk):
            pl.semaphore_signal(barrier, inc=1, device_id=(g, blk_peer(step)), device_id_type=MESH)

    first = [load(features, feat, in_sems.at[0]), load(col_scale, cscale, in_sems.at[1])]

    cols_load = load(cols_in, cols, in_sems.at[6])

    tile_loads = []
    for spot, step in enumerate(order):
        rows = pl.ds(blk_peer(step) * TPR, TPR)
        tile_loads.append(load(tiles.at[rows], held.at[rows], tile_sems.at[spot]))
    late = [
        load(row_scale, rscale, in_sems.at[2]),
        load(train_mask, mask, in_sems.at[3]),
        load(weight, wgt, in_sems.at[4]),
        load(cotangent, cot, in_sems.at[5]),
    ]

    for copy in first:
        copy.wait()
    sources[g] = (down_rows(cscale[...], feat.shape[1]) * feat[...].astype(F32)).astype(BF16)
    if near:
        pl.semaphore_wait(barrier, n_grp - 1 + greeters)
    else:
        pl.semaphore_wait(barrier, n_grp + n_blk - 2)

    src_copies = []
    for step in range(1, n_grp):
        copy = pltpu.make_async_remote_copy(
            src_ref=sources.at[g], dst_ref=sources.at[g],
            send_sem=src_send.at[step - 1], recv_sem=src_recv.at[step - 1],
            device_id=(grp_peer(step), b), device_id_type=MESH)
        copy.start()
        src_copies.append(copy)
    if near:
        greet(greet_sems.at[0])
        pl.semaphore_wait(greet_sems.at[0], greeters)
        pl.semaphore_signal(greet_sems.at[1], inc=1, device_id=(g, flip(b, 4)), device_id_type=MESH)
        pl.semaphore_wait(greet_sems.at[1], 1)
    cols_load.wait()
    for copy in tile_loads:
        copy.wait()
    for copy in late:
        copy.wait()
    row_full = down_rows(rscale[...], feat.shape[1])
    mask_full = down_rows(mask[...].astype(F32), cot.shape[1] // 2)
    masked = cot[...].astype(F32) * jnp.concatenate([mask_full, mask_full], axis=1)

    for copy in src_copies:
        copy.wait_recv()

    def partial(block):
        base = block * TPR
        left = jnp.concatenate([held[base + k] for k in range(TPR)], axis=1)
        right = jnp.concatenate([sources[cols[base + k]] for k in range(TPR)], axis=0)
        return jnp.dot(left, right, preferred_element_type=F32)

    middle = (row > 0) & (row < last_row)
    crossed, straight = order.index(5), order.index(4)
    tile = feat.shape[0]

    def spread(cut):
        copies = []
        upper, lower, rest = pl.ds(0, cut), pl.ds(cut, tile - cut), pl.ds(0, tile - cut)

        def pass_on(source, target, slot, sem, to):
            copy = pltpu.make_async_remote_copy(
                src_ref=source, dst_ref=target, send_sem=part_send.at[slot],
                recv_sem=sem, device_id=(g, to), device_id_type=MESH)
            copy.start()
            copies.append(copy)

        if near:
            outgoing[crossed] = partial(blk_peer(5)).astype(BF16)
            pass_on(outgoing.at[crossed, lower], handed.at[rest], n_blk - 1, hand_sem.at[0], blk_peer(1))
        for spot, step in enumerate(order[:-1]):
            block = blk_peer(step)
            if near and spot == straight:
                part = partial(block)
                outgoing[spot, :cut] = part[:cut].astype(BF16)
                kept[:tile - cut] = part[cut:]
            elif not near or spot != crossed:
                outgoing[spot] = partial(block).astype(BF16)
            rows = upper if near and step in (4, 5) else pl.ds(0, tile)
            pass_on(outgoing.at[spot, rows], arrived.at[b, rows], spot, part_recv.at[b], block)
        mine[...] = partial(b)
        if near:
            @pl.when(middle)
            def _():
                for step in (5, 7):
                    arrived[blk_peer(step), cut:] = jnp.zeros((tile - cut, feat.shape[1]), BF16)

            pltpu.make_async_copy(handed.at[rest], handed.at[rest], hand_sem.at[0]).wait()
            outgoing[straight, cut:] = (kept[:tile - cut] + handed[:tile - cut].astype(F32)).astype(BF16)
            pass_on(outgoing.at[straight, lower], arrived.at[b, lower], n_blk, part_recv.at[b], blk_peer(4))
        for step in (1, 2, 3, 5, 7, 6, 4) if near else reversed(order[:-1]):
            block = blk_peer(step)

            def landed(rows, block=block):
                slot = arrived.at[block, pl.ds(0, rows)]
                pltpu.make_async_copy(slot, slot, part_recv.at[block]).wait()

            if near and step in (5, 7):
                pl.when(jnp.logical_not(middle))(functools.partial(landed, tile))
                pl.when(middle)(functools.partial(landed, cut))
            else:
                landed(tile)
        for copy in copies:
            copy.wait_send()

    if near:
        pl.when(lax.rem(g, 2) == 0)(functools.partial(spread, CUTS[0]))
        pl.when(lax.rem(g, 2) == 1)(functools.partial(spread, CUTS[1]))
    else:
        spread(tile)

    total = mine[...]
    for step in (1, 2, 3, 5, 7, 6, 4) if near else reversed(order[:-1]):
        total = total + arrived[blk_peer(step)].astype(F32)
    mixed = row_full * total

    high, low = split(mixed)
    w = wgt[...]
    pre = jnp.dot(jnp.concatenate([high, low], axis=1), jnp.concatenate([w, w], axis=0),
                  preferred_element_type=F32)
    square = pre * pre
    bent = jnp.tanh(ROOT * pre * (1.0 + CUBE * square))
    half = 0.5 * (1.0 + bent)
    hidden = (pre * half).astype(BF16).astype(packed.dtype)
    slope = half + 0.5 * pre * (1.0 - bent * bent) * (ROOT * (1.0 + 3.0 * CUBE * square))
    delta = slope * masked

    high_t, low_t = split(mixed.T)
    d_high, d_low = split(delta)
    grad = jnp.dot(jnp.concatenate([high_t, low_t, high_t], axis=1),
                   jnp.concatenate([d_high, d_high, d_low], axis=0), preferred_element_type=F32)
    if not near:
        packed[:top] = hidden
        packed[top:] = grad
        for copy in src_copies:
            copy.wait_send()
        return

    owners, senders = grad_parts.shape[0], grad_in.shape[0]
    floor, core = g // 2, lax.rem(g, 2)
    owner = (row > 0) & (row < last_row) & (core == 1)
    me = g * n_blk + b
    for piece in range(owners):
        grad_parts[piece] = grad[piece * deep:piece * deep + deep].astype(BF16)

    for mid in (1 - hemi, hemi):
        for turn in reversed(range(4)):
            to_floor, to_side = lax.rem(floor + turn // 2, 2), lax.rem(side + turn, 2)
            to_g, to_b = 2 * to_floor + 1, 2 * (1 + mid) + to_side

            def scatter(to_g=to_g, to_b=to_b, to_seat=4 * mid + 2 * to_floor + to_side):
                pltpu.make_async_remote_copy(
                    src_ref=grad_parts.at[to_seat], dst_ref=grad_in.at[me],
                    send_sem=grad_sems.at[0], recv_sem=grad_sems.at[1],
                    device_id=(to_g, to_b), device_id_type=MESH).start()

            if turn == 0:
                pl.when((to_g != g) | (to_b != b))(scatter)
            else:
                scatter()
    packed[:top] = hidden
    for copy in src_copies:
        copy.wait_send()
    gradient = packed.at[pl.ds(top, owners * deep)]

    @pl.when(owner)
    def _():
        seat = 4 * hemi + 2 * floor + side
        grad_in[me] = grad_parts[seat]
        others, some = grad_in.at[pl.ds(0, senders - 1)], grad_parts.at[pl.ds(0, owners - 1)]
        pltpu.make_async_copy(others, others, grad_sems.at[1]).wait()
        own = pl.ds(pl.multiple_of(top + seat * deep, deep), deep)
        packed[own] = jnp.sum(grad_in[...].astype(F32), axis=0).astype(BF16)
        for row_to in ROWS:
            for turn in range(2 * n_grp):
                to_g, to_b = turn % n_grp, 2 * row_to + turn // n_grp

                def gather(to_g=to_g, to_b=to_b):
                    pltpu.make_async_remote_copy(
                        src_ref=packed.at[own], dst_ref=packed.at[own],
                        send_sem=grad_sems.at[2], recv_sem=grad_sems.at[3],
                        device_id=(to_g, to_b), device_id_type=MESH).start()

                if row_to in (1, 2) and to_g % 2:
                    pl.when((to_g != g) | (to_b != b))(gather)
                else:
                    gather()
        pltpu.make_async_copy(some, some, grad_sems.at[0]).wait()
        rest = packed.at[pl.ds(top, (owners - 1) * deep)]
        pltpu.make_async_copy(rest, rest, grad_sems.at[3]).wait()
        pltpu.make_async_copy(others, others, grad_sems.at[2]).wait()

    @pl.when(jnp.logical_not(owner))
    def _():
        pltpu.make_async_copy(grad_parts, grad_parts, grad_sems.at[0]).wait()
        pltpu.make_async_copy(gradient, gradient, grad_sems.at[3]).wait()


def shards(n_grp, n_blk, features, col_scale, row_scale, tiles, tile_cols, weight, cotangent, train_mask):
    nodes, fin = features.shape
    hid_width = weight.shape[1]
    tile = tiles.shape[1]
    near = n_grp == 4 and n_blk == 8 and fin == 128
    hbm = pl.BlockSpec(memory_space=pltpu.HBM)
    deep = 16 if near else 8
    spare = (fin // deep if near else 1, deep, hid_width)
    landing = (n_grp * n_blk if near else 1, deep, hid_width)
    out_type = BF16 if near else F32
    dma = pltpu.SemaphoreType.DMA
    packed = pl.pallas_call(
        functools.partial(kernel, n_grp, n_blk, near),
        out_shape=pltpu.VMEM((nodes + fin, hid_width), out_type),
        in_specs=[hbm] * 8,
        out_specs=pl.BlockSpec(memory_space=pltpu.VMEM),
        scratch_shapes=[
            pltpu.SMEM(tile_cols.shape, jnp.int32),
            pltpu.VMEM((nodes, fin), BF16),
            pltpu.VMEM((1, nodes), F32),
            pltpu.VMEM((1, nodes), F32),
            pltpu.VMEM((1, nodes), jnp.int32),
            pltpu.VMEM((fin, hid_width), BF16),
            pltpu.VMEM((nodes, hid_width), BF16),
            pltpu.VMEM(tiles.shape, BF16),
            pltpu.VMEM((n_grp, tile, fin), BF16),
            pltpu.VMEM((tile, fin), F32),
            pltpu.VMEM((n_blk - 1, tile, fin), BF16),
            pltpu.VMEM((n_blk, tile, fin), BF16),
            pltpu.VMEM(spare, BF16),
            pltpu.VMEM(landing, BF16),
            dma((7,)), dma((n_blk,)), dma((n_grp - 1,)), dma((n_grp - 1,)),
            dma((n_blk + 1,)), dma((n_blk,)), dma((4,)),
            pltpu.SemaphoreType.REGULAR((2,)),
            pltpu.VMEM((tile - min(CUTS), fin), BF16), pltpu.VMEM((tile - min(CUTS), fin), F32), dma((1,)),
        ],
        compiler_params=pltpu.CompilerParams(
            collective_id=0, has_side_effects=True, vmem_limit_bytes=VLIM),
    )(*[pltpu.with_memory_space_constraint(x, pltpu.HBM) for x in (
        tile_cols, features, col_scale.reshape(1, nodes), row_scale.reshape(1, nodes), tiles, weight,
        cotangent, train_mask.reshape(1, nodes))])
    hidden, grad = packed[:nodes].astype(BF16), packed[nodes:].astype(F32)
    if not near:
        grad = lax.psum(grad, ("grp", "blk"))
    return hidden, grad


def solution(mesh):
    in_specs = (
        P(("grp", "blk"), None),
        P(("grp", "blk")),
        P(("grp", "blk")),
        P(("grp", "blk"), None, None),
        P(("grp", "blk")),
        P(),
        P(("grp", "blk"), None),
        P(("grp", "blk")),
    )
    out_specs = (P(("grp", "blk"), None), P())
    body = functools.partial(shards, mesh.shape["grp"], mesh.shape["blk"])
    return jax.shard_map(body, mesh=mesh, in_specs=in_specs, out_specs=out_specs, check_vma=False)
```

```python
import functools
import math

import jax
import jax.numpy as jnp
from jax import lax
from jax.experimental import pallas as pl
from jax.experimental.pallas import tpu as pltpu
from jax.sharding import PartitionSpec as P

TPR = 4
ROOT = math.sqrt(2.0 / math.pi)
CUBE = 0.044715
MESH = pl.DeviceIdType.MESH
F32 = jnp.float32
BF16 = jnp.bfloat16
VLIM = 32 * 1024 * 1024
CUTS = (48, 16)
ROWS = (0, 3, 2, 1)


def far_first(count):
    return sorted(range(1, count), key=lambda step: abs(2 * step - count))


def split(value):
    high = value.astype(BF16)
    return high, (value - high.astype(F32)).astype(BF16)


def down_rows(row, width):
    return jnp.broadcast_to(row, (width, row.shape[1])).T


def kernel(n_grp, n_blk, near, cols_in, features, col_scale, row_scale, tiles, weight, cotangent,
           train_mask, packed, cols, feat, cscale, rscale, mask, wgt, cot, held, sources,
           mine, outgoing, arrived, grad_parts, grad_in, in_sems, tile_sems, src_send,
           src_recv, part_send, part_recv, grad_sems, greet_sems,
           handed, kept, hand_sem):
    deep, hid_width = grad_parts.shape[1], packed.shape[1]
    top = feat.shape[0]
    g, b = lax.axis_index("grp"), lax.axis_index("blk")
    last_row = n_blk // 2 - 1
    row, side = b // 2, lax.rem(b, 2)
    order = list(range(n_blk - 1, -1, -1)) if near else far_first(n_blk) + [0]

    def flip(index, mask):
        out, weight = 0, 1
        while weight <= mask:
            bit = lax.rem(index // weight, 2)
            out = out + weight * (1 - 2 * bit) * (mask // weight % 2)
            weight *= 2
        return index + out

    def grp_peer(step):
        return flip(g, step) if near else lax.rem(g + step, n_grp)

    hemi = row // 2
    rows_near = (row, row + 1 - 2 * lax.rem(row, 2), 2 - hemi, 3 * (1 - hemi))

    def blk_peer(step):
        if near:
            return 2 * rows_near[step // 2] + (1 - side if step % 2 else side)
        return lax.rem(b + step, n_blk)

    def load(source, target, sem):
        copy = pltpu.make_async_copy(source, target, sem)
        copy.start()
        return copy

    def greet(sem):
        pl.semaphore_signal(sem, inc=1, device_id=(g, b + 1 - 2 * side), device_id_type=MESH)

        @pl.when(row > 0)
        def _():
            pl.semaphore_signal(sem, inc=1, device_id=(g, b - 2), device_id_type=MESH)

        @pl.when(row < last_row)
        def _():
            pl.semaphore_signal(sem, inc=1, device_id=(g, b + 2), device_id_type=MESH)

    greeters = 1 + jnp.minimum(row, 1) + jnp.minimum(last_row - row, 1)

    barrier = pltpu.get_barrier_semaphore()
    if near:
        greet(barrier)
    for step in reversed(range(1, n_grp)):
        pl.semaphore_signal(barrier, inc=1, device_id=(grp_peer(step), b), device_id_type=MESH)
    if not near:
        for step in range(1, n_blk):
            pl.semaphore_signal(barrier, inc=1, device_id=(g, blk_peer(step)), device_id_type=MESH)

    first = [load(features, feat, in_sems.at[0]), load(col_scale, cscale, in_sems.at[1])]

    cols_load = load(cols_in, cols, in_sems.at[6])

    tile_loads = []
    for spot, step in enumerate(order):
        rows = pl.ds(blk_peer(step) * TPR, TPR)
        tile_loads.append(load(tiles.at[rows], held.at[rows], tile_sems.at[spot]))
    late = [
        load(row_scale, rscale, in_sems.at[2]),
        load(train_mask, mask, in_sems.at[3]),
        load(weight, wgt, in_sems.at[4]),
        load(cotangent, cot, in_sems.at[5]),
    ]

    for copy in first:
        copy.wait()
    sources[g] = (down_rows(cscale[...], feat.shape[1]) * feat[...].astype(F32)).astype(BF16)
    if near:
        pl.semaphore_wait(barrier, n_grp - 1 + greeters)
    else:
        pl.semaphore_wait(barrier, n_grp + n_blk - 2)

    src_copies = []
    for step in range(1, n_grp):
        copy = pltpu.make_async_remote_copy(
            src_ref=sources.at[g], dst_ref=sources.at[g],
            send_sem=src_send.at[step - 1], recv_sem=src_recv.at[step - 1],
            device_id=(grp_peer(step), b), device_id_type=MESH)
        copy.start()
        src_copies.append(copy)
    if near:
        greet(greet_sems.at[0])
        pl.semaphore_wait(greet_sems.at[0], greeters)
        pl.semaphore_signal(greet_sems.at[1], inc=1, device_id=(g, flip(b, 4)), device_id_type=MESH)
        pl.semaphore_wait(greet_sems.at[1], 1)
    cols_load.wait()
    for copy in tile_loads:
        copy.wait()
    for copy in late:
        copy.wait()
    row_full = down_rows(rscale[...], feat.shape[1])
    mask_full = down_rows(mask[...].astype(F32), cot.shape[1] // 2)
    masked = cot[...].astype(F32) * jnp.concatenate([mask_full, mask_full], axis=1)

    for copy in src_copies:
        copy.wait_recv()

    def partial(block):
        base = block * TPR
        left = jnp.concatenate([held[base + k] for k in range(TPR)], axis=1)
        right = jnp.concatenate([sources[cols[base + k]] for k in range(TPR)], axis=0)
        return jnp.dot(left, right, preferred_element_type=F32)

    middle = (row > 0) & (row < last_row)
    crossed, straight = order.index(5), order.index(4)
    tile = feat.shape[0]

    def spread(cut):
        copies = []
        upper, lower, rest = pl.ds(0, cut), pl.ds(cut, tile - cut), pl.ds(0, tile - cut)

        def pass_on(source, target, slot, sem, to):
            copy = pltpu.make_async_remote_copy(
                src_ref=source, dst_ref=target, send_sem=part_send.at[slot],
                recv_sem=sem, device_id=(g, to), device_id_type=MESH)
            copy.start()
            copies.append(copy)

        if near:
            outgoing[crossed] = partial(blk_peer(5)).astype(BF16)
            pass_on(outgoing.at[crossed, lower], handed.at[rest], n_blk - 1, hand_sem.at[0], blk_peer(1))
        for spot, step in enumerate(order[:-1]):
            block = blk_peer(step)
            if near and spot == straight:
                part = partial(block)
                outgoing[spot, :cut] = part[:cut].astype(BF16)
                kept[:tile - cut] = part[cut:]
            elif not near or spot != crossed:
                outgoing[spot] = partial(block).astype(BF16)
            rows = upper if near and step in (4, 5) else pl.ds(0, tile)
            pass_on(outgoing.at[spot, rows], arrived.at[b, rows], spot, part_recv.at[b], block)
        mine[...] = partial(b)
        if near:
            @pl.when(middle)
            def _():
                for step in (5, 7):
                    arrived[blk_peer(step), cut:] = jnp.zeros((tile - cut, feat.shape[1]), BF16)

            pltpu.make_async_copy(handed.at[rest], handed.at[rest], hand_sem.at[0]).wait()
            outgoing[straight, cut:] = (kept[:tile - cut] + handed[:tile - cut].astype(F32)).astype(BF16)
            pass_on(outgoing.at[straight, lower], arrived.at[b, lower], n_blk, part_recv.at[b], blk_peer(4))
        for step in (1, 2, 3, 5, 7, 6, 4) if near else reversed(order[:-1]):
            block = blk_peer(step)

            def landed(rows, block=block):
                slot = arrived.at[block, pl.ds(0, rows)]
                pltpu.make_async_copy(slot, slot, part_recv.at[block]).wait()

            if near and step in (5, 7):
                pl.when(jnp.logical_not(middle))(functools.partial(landed, tile))
                pl.when(middle)(functools.partial(landed, cut))
            else:
                landed(tile)
        if not near:
            for copy in copies:
                copy.wait_send()

    def drained(cut):
        for spot, step in enumerate(order[:-1]):
            left = outgoing.at[spot, pl.ds(0, cut if step in (4, 5) else tile)]
            pltpu.make_async_copy(left, left, part_send.at[spot]).wait()
        for slot in (n_blk - 1, n_blk):
            left = outgoing.at[crossed, pl.ds(cut, tile - cut)]
            pltpu.make_async_copy(left, left, part_send.at[slot]).wait()

    if near:
        pl.when(lax.rem(g, 2) == 0)(functools.partial(spread, CUTS[0]))
        pl.when(lax.rem(g, 2) == 1)(functools.partial(spread, CUTS[1]))
    else:
        spread(tile)

    total = mine[...]
    for step in (1, 2, 3, 5, 7, 6, 4) if near else reversed(order[:-1]):
        total = total + arrived[blk_peer(step)].astype(F32)
    mixed = row_full * total

    high, low = split(mixed)
    w = wgt[...]
    pre = jnp.dot(jnp.concatenate([high, low], axis=1), jnp.concatenate([w, w], axis=0),
                  preferred_element_type=F32)
    square = pre * pre
    bent = jnp.tanh(ROOT * pre * (1.0 + CUBE * square))
    half = 0.5 * (1.0 + bent)
    hidden = (pre * half).astype(BF16).astype(packed.dtype)
    slope = half + 0.5 * pre * (1.0 - bent * bent) * (ROOT * (1.0 + 3.0 * CUBE * square))
    delta = slope * masked

    high_t, low_t = split(mixed.T)
    d_high, d_low = split(delta)
    grad = jnp.dot(jnp.concatenate([high_t, low_t, high_t], axis=1),
                   jnp.concatenate([d_high, d_high, d_low], axis=0), preferred_element_type=F32)
    if not near:
        packed[:top] = hidden
        packed[top:] = grad
        for copy in src_copies:
            copy.wait_send()
        return

    owners, senders = grad_parts.shape[0], grad_in.shape[0]
    floor, core = g // 2, lax.rem(g, 2)
    owner = (row > 0) & (row < last_row) & (core == 1)
    me = g * n_blk + b
    for piece in range(owners):
        grad_parts[piece] = grad[piece * deep:piece * deep + deep].astype(BF16)

    for mid in (1 - hemi, hemi):
        for turn in reversed(range(4)):
            to_floor, to_side = lax.rem(floor + turn // 2, 2), lax.rem(side + turn, 2)
            to_g, to_b = 2 * to_floor + 1, 2 * (1 + mid) + to_side

            def scatter(to_g=to_g, to_b=to_b, to_seat=4 * mid + 2 * to_floor + to_side):
                pltpu.make_async_remote_copy(
                    src_ref=grad_parts.at[to_seat], dst_ref=grad_in.at[me],
                    send_sem=grad_sems.at[0], recv_sem=grad_sems.at[1],
                    device_id=(to_g, to_b), device_id_type=MESH).start()

            if turn == 0:
                pl.when((to_g != g) | (to_b != b))(scatter)
            else:
                scatter()
    packed[:top] = hidden
    for copy in src_copies:
        copy.wait_send()
    pl.when(core == 0)(functools.partial(drained, CUTS[0]))
    pl.when(core == 1)(functools.partial(drained, CUTS[1]))
    gradient = packed.at[pl.ds(top, owners * deep)]

    @pl.when(owner)
    def _():
        seat = 4 * hemi + 2 * floor + side
        grad_in[me] = grad_parts[seat]
        others, some = grad_in.at[pl.ds(0, senders - 1)], grad_parts.at[pl.ds(0, owners - 1)]
        pltpu.make_async_copy(others, others, grad_sems.at[1]).wait()
        own = pl.ds(pl.multiple_of(top + seat * deep, deep), deep)
        packed[own] = jnp.sum(grad_in[...].astype(F32), axis=0).astype(BF16)
        for row_to in ROWS:
            for turn in range(2 * n_grp):
                to_g, to_b = turn % n_grp, 2 * row_to + turn // n_grp

                def gather(to_g=to_g, to_b=to_b):
                    pltpu.make_async_remote_copy(
                        src_ref=packed.at[own], dst_ref=packed.at[own],
                        send_sem=grad_sems.at[2], recv_sem=grad_sems.at[3],
                        device_id=(to_g, to_b), device_id_type=MESH).start()

                if row_to in (1, 2) and to_g % 2:
                    pl.when((to_g != g) | (to_b != b))(gather)
                else:
                    gather()
        pltpu.make_async_copy(some, some, grad_sems.at[0]).wait()
        rest = packed.at[pl.ds(top, (owners - 1) * deep)]
        pltpu.make_async_copy(rest, rest, grad_sems.at[3]).wait()
        pltpu.make_async_copy(others, others, grad_sems.at[2]).wait()

    @pl.when(jnp.logical_not(owner))
    def _():
        pltpu.make_async_copy(grad_parts, grad_parts, grad_sems.at[0]).wait()
        pltpu.make_async_copy(gradient, gradient, grad_sems.at[3]).wait()


def shards(n_grp, n_blk, features, col_scale, row_scale, tiles, tile_cols, weight, cotangent, train_mask):
    nodes, fin = features.shape
    hid_width = weight.shape[1]
    tile = tiles.shape[1]
    near = n_grp == 4 and n_blk == 8 and fin == 128
    hbm = pl.BlockSpec(memory_space=pltpu.HBM)
    deep = 16 if near else 8
    spare = (fin // deep if near else 1, deep, hid_width)
    landing = (n_grp * n_blk if near else 1, deep, hid_width)
    out_type = BF16 if near else F32
    dma = pltpu.SemaphoreType.DMA
    packed = pl.pallas_call(
        functools.partial(kernel, n_grp, n_blk, near),
        out_shape=pltpu.VMEM((nodes + fin, hid_width), out_type),
        in_specs=[hbm] * 8,
        out_specs=pl.BlockSpec(memory_space=pltpu.VMEM),
        scratch_shapes=[
            pltpu.SMEM(tile_cols.shape, jnp.int32),
            pltpu.VMEM((nodes, fin), BF16),
            pltpu.VMEM((1, nodes), F32),
            pltpu.VMEM((1, nodes), F32),
            pltpu.VMEM((1, nodes), jnp.int32),
            pltpu.VMEM((fin, hid_width), BF16),
            pltpu.VMEM((nodes, hid_width), BF16),
            pltpu.VMEM(tiles.shape, BF16),
            pltpu.VMEM((n_grp, tile, fin), BF16),
            pltpu.VMEM((tile, fin), F32),
            pltpu.VMEM((n_blk - 1, tile, fin), BF16),
            pltpu.VMEM((n_blk, tile, fin), BF16),
            pltpu.VMEM(spare, BF16),
            pltpu.VMEM(landing, BF16),
            dma((7,)), dma((n_blk,)), dma((n_grp - 1,)), dma((n_grp - 1,)),
            dma((n_blk + 1,)), dma((n_blk,)), dma((4,)),
            pltpu.SemaphoreType.REGULAR((2,)),
            pltpu.VMEM((tile - min(CUTS), fin), BF16), pltpu.VMEM((tile - min(CUTS), fin), F32), dma((1,)),
        ],
        compiler_params=pltpu.CompilerParams(
            collective_id=0, has_side_effects=True, vmem_limit_bytes=VLIM),
    )(*[pltpu.with_memory_space_constraint(x, pltpu.HBM) for x in (
        tile_cols, features, col_scale.reshape(1, nodes), row_scale.reshape(1, nodes), tiles, weight,
        cotangent, train_mask.reshape(1, nodes))])
    hidden, grad = packed[:nodes].astype(BF16), packed[nodes:].astype(F32)
    if not near:
        grad = lax.psum(grad, ("grp", "blk"))
    return hidden, grad


def solution(mesh):
    in_specs = (
        P(("grp", "blk"), None),
        P(("grp", "blk")),
        P(("grp", "blk")),
        P(("grp", "blk"), None, None),
        P(("grp", "blk")),
        P(),
        P(("grp", "blk"), None),
        P(("grp", "blk")),
    )
    out_specs = (P(("grp", "blk"), None), P())
    body = functools.partial(shards, mesh.shape["grp"], mesh.shape["blk"])
    return jax.shard_map(body, mesh=mesh, in_specs=in_specs, out_specs=out_specs, check_vma=False)
```
